128 devices in a mesh: cell: 4 (over x), energy: 32 (over y, z, core).
Axes of the slice: x: 4, y: 4, z: 4, core: 2. Of those that a mesh axis runs over, the one named last changes fastest.
Arguments:
- hamiltonian: float32 [4, 2, 128, 128], P('cell'), may hold values from -2 to 2, as said below
- coupling: float32 [4, 2, 128, 128], P('cell'), may hold values from -0.25 to 0.25
- sigma_in: float32 [4, 128, 2, 128, 128], P('cell', 'energy'), may hold values from -1 to 1, as said below
- mode_offsets: int32 [4], replicated, may hold values from 1 to 8, as said below
- mode_coupling: float32 [4], replicated, may hold values from 0.1 to 0.4
- energy_owner: int32 [128], replicated, may hold values from 0 to 127, as said below
Outputs:
- green_diag: float32 [4, 128, 2, 128, 128], P('cell', 'energy')
- sigma_out: float32 [4, 128, 2, 128, 128], P('cell', 'energy')
The draws below stay inside these ranges and needn't reach their ends.
Inputs may be any that keep to these rules, and one draw needn't show every extreme that they name: `hamiltonian`: every block is Hermitian. `sigma_in`: the anti-Hermitian part of every block is negative semidefinite. `energy_owner`: every energy index stands in exactly one slot; slot s holds an index from 4 * (s // 4) to 4 * (s // 4) + 3. `mode_offsets`: some mode has offset exactly 8.
All inputs are finite; a program needn't handle non-finite values.
Results may differ from the reference program's by a relative error of at most 0.00011.
Values sent between devices are 32-bit elements; how exact they have to be, the bound alone decides.
A program may use at most 64 MiB of HBM per device.

```python
import math
import jax
import jax.numpy as jnp
from jax import lax

B = 128
E_DEV = 4
MODES = 4
OFFSET_MAX = 8
NC = 4
NE = 128


def draw_hamiltonian(key, part):
    keys = jax.random.split(key, 3)
    coupled = jax.random.uniform(keys[0], (NC, B, B), jnp.float32, -1.0, 1.0)
    onsite = jax.random.uniform(keys[2], (NC, B), jnp.float32, -1.0, 1.0)
    twisted = jax.random.uniform(keys[1], (NC, B, B), jnp.float32, -1.0, 1.0)
    scale = 0.9 / jnp.sqrt(jnp.float32(B))
    identity = jnp.eye(B, dtype=jnp.float32)
    real_part = (coupled + jnp.swapaxes(coupled, -1, -2)) * scale + onsite[:, :, None] * identity
    imag_part = (twisted - jnp.swapaxes(twisted, -1, -2)) * (0.4 / jnp.sqrt(jnp.float32(B)))
    return jnp.stack([real_part, imag_part], axis=1)


def draw_sigma_in(key, part):
    keys = jax.random.split(key, 4)
    shape = (NC, NE, B, B)
    first_real = jax.random.uniform(keys[0], shape, jnp.float32, -1.7, 1.7)
    first_imag = jax.random.uniform(keys[1], shape, jnp.float32, -1.7, 1.7)
    precise = lax.Precision.HIGHEST
    swap_real = jnp.swapaxes(first_real, -1, -2)
    swap_imag = jnp.swapaxes(first_imag, -1, -2)
    factor = 0.05 / B
    pos_real = (jnp.matmul(first_real, swap_real, precision=precise) + jnp.matmul(first_imag, swap_imag, precision=precise)) * factor
    pos_imag = (jnp.matmul(first_imag, swap_real, precision=precise) - jnp.matmul(first_real, swap_imag, precision=precise)) * factor
    herm_real = jax.random.uniform(keys[2], shape, jnp.float32, -1.0, 1.0)
    herm_imag = jax.random.uniform(keys[3], shape, jnp.float32, -1.0, 1.0)
    spread = 0.1 / jnp.sqrt(jnp.float32(B))
    real_part = (herm_real + jnp.swapaxes(herm_real, -1, -2)) * spread + pos_imag
    imag_part = (herm_imag - jnp.swapaxes(herm_imag, -1, -2)) * spread - pos_real
    return jnp.stack([real_part, imag_part], axis=2)


def draw_mode_offsets(key, part):
    keys = jax.random.split(jax.random.fold_in(key, 17), 2)
    offsets = jax.random.randint(keys[0], (MODES,), 1, OFFSET_MAX + 1)
    chosen = jax.random.randint(keys[1], (), 0, MODES)
    return jnp.where(jnp.arange(MODES) == chosen, OFFSET_MAX, offsets).astype(jnp.int32)


def draw_energy_owner(key, part):
    block_count = NE // E_DEV
    keys = jax.random.split(jax.random.fold_in(key, 29), block_count)
    orders = jax.vmap(lambda one_key: jax.random.permutation(one_key, E_DEV))(keys)
    starts = jnp.arange(block_count, dtype=jnp.int32)[:, None] * E_DEV
    return (orders.astype(jnp.int32) + starts).reshape(NE).astype(jnp.int32)


def shard_levels(key, shape, shards, low, largest):
    loudness, own = 1.0, jax.random.fold_in(key, 6)
    for axis_at, shards_of in shards:
        steps = jnp.exp(jax.random.uniform(jax.random.fold_in(own, axis_at), (shards_of,), jnp.float32, low / len(shards), largest / len(shards)))
        loudness = loudness * jnp.repeat(steps, shape[axis_at] // shards_of).reshape([-1 if axis == axis_at else 1 for axis in range(len(shape))])
    return loudness


def scatter_about(rng, dims, scale, most, cuts=(), held_as=jnp.bfloat16):
    factor_of = shard_levels(rng, dims, cuts, -0.22, 0.18) if cuts else 1.0
    values = jax.random.normal(rng, dims, jnp.float32) * scale * factor_of
    return jnp.minimum(jnp.maximum(values, -most), most).astype(held_as)


def setup_inputs(seed: int = 0) -> dict:
    key_list = jax.random.split(jax.random.key(seed), 7)
    return {
        "hamiltonian": draw_hamiltonian(jax.random.fold_in(key_list[6], 71), 0),
        "coupling": scatter_about(key_list[1], (NC, 2, B, B), (4 * B) ** -0.5, 0.25, ((0, 4),), jnp.float32),
        "sigma_in": draw_sigma_in(jax.random.fold_in(key_list[6], 71), 0),
        "mode_offsets": draw_mode_offsets(jax.random.fold_in(key_list[6], 71), 0),
        "mode_coupling": jnp.clip(jnp.exp(jax.random.uniform(key_list[4], (MODES,), jnp.float32, math.log(0.1), math.log(0.4))), 0.1, 0.4),
        "energy_owner": draw_energy_owner(jax.random.fold_in(key_list[6], 71), 0),
    }


PRECISE = lax.Precision.HIGHEST
BROADENING = 0.2
CONTACT_RATE = 0.5
LEAD_WIDTH = 1.0
BAND_LOW = -2.5
BAND_SPAN = 5.0

def complex_product(first, second):
    first_real, first_imag = (first[..., 0, :, :], first[..., 1, :, :])
    second_real, second_imag = (second[..., 0, :, :], second[..., 1, :, :])
    real_part = jnp.matmul(first_real, second_real, precision=PRECISE) - jnp.matmul(first_imag, second_imag, precision=PRECISE)
    imag_part = jnp.matmul(first_real, second_imag, precision=PRECISE) + jnp.matmul(first_imag, second_real, precision=PRECISE)
    return jnp.stack([real_part, imag_part], axis=-3)

def adjoint(matrix):
    return jnp.stack([jnp.swapaxes(matrix[..., 0, :, :], -1, -2), -jnp.swapaxes(matrix[..., 1, :, :], -1, -2)], axis=-3)

def invert(matrix):
    real_part, imag_part = (matrix[..., 0, :, :], matrix[..., 1, :, :])
    orbitals = matrix.shape[-1]
    embedded = jnp.concatenate([jnp.concatenate([real_part, -imag_part], -1), jnp.concatenate([imag_part, real_part], -1)], -2)
    identity = jnp.eye(orbitals, dtype=matrix.dtype)
    columns = jnp.concatenate([identity, jnp.zeros_like(identity)], 0)
    columns = jnp.broadcast_to(columns, embedded.shape[:-1] + (orbitals,))
    solution = jnp.linalg.solve(embedded, columns)
    return jnp.stack([solution[..., :orbitals, :], solution[..., orbitals:, :]], axis=-3)

def reference(hamiltonian, coupling, sigma_in, mode_offsets, mode_coupling, energy_owner):
    orbitals = hamiltonian.shape[-1]
    cell_count = hamiltonian.shape[0]
    energy_count = sigma_in.shape[1]
    float_type = hamiltonian.dtype
    identity = jnp.eye(orbitals, dtype=float_type)
    nothing = jnp.zeros_like(identity)
    contact = jnp.stack([nothing, -CONTACT_RATE * identity])
    lead_green = jnp.stack([nothing, -LEAD_WIDTH * identity])
    levels = BAND_LOW + BAND_SPAN * energy_owner.astype(float_type) / (energy_count - 1)

    def one_energy(inputs):
        energy_level, self_energy = inputs
        diagonal_part = jnp.stack([energy_level * identity, BROADENING * identity])
        shifted = diagonal_part[None] - hamiltonian - self_energy
        left_terms = []
        schur_term = contact
        for local_cell in range(cell_count):
            left_terms.append(schur_term)
            partial_green = invert(shifted[local_cell] - schur_term)
            schur_term = complex_product(adjoint(coupling[local_cell]), complex_product(partial_green, coupling[local_cell]))
        right_terms = [None] * cell_count
        partial_green = lead_green
        for local_cell in reversed(range(cell_count)):
            schur_term = complex_product(coupling[local_cell], complex_product(partial_green, adjoint(coupling[local_cell])))
            right_terms[local_cell] = schur_term
            partial_green = invert(shifted[local_cell] - schur_term)
        return invert(shifted - jnp.stack(left_terms) - jnp.stack(right_terms))
    green_energy = lax.map(one_energy, (levels, jnp.swapaxes(sigma_in, 0, 1)))
    offset_table = energy_owner[None, :] - energy_owner[:, None]
    matches = (offset_table[:, :, None] == -mode_offsets).astype(float_type) + (offset_table[:, :, None] == mode_offsets).astype(float_type)
    weights = jnp.sum(matches * mode_coupling, -1)

    def one_cell(cell_green):
        flat = cell_green.reshape(energy_count, -1)
        return jnp.dot(weights, flat, precision=PRECISE).reshape(cell_green.shape)
    sigma_out = lax.map(one_cell, jnp.swapaxes(green_energy, 0, 1))
    return (jnp.swapaxes(green_energy, 0, 1), sigma_out)
```

```python
import jax
import jax.numpy as jnp
from jax import lax
from jax.experimental import pallas as pl
from jax.experimental.pallas import tpu as pltpu
from jax.sharding import PartitionSpec as P

OFFSET_MAX = 8

PRECISE = lax.Precision.HIGHEST
BROADENING = 0.2
CONTACT_RATE = 0.5
LEAD_WIDTH = 1.0
BAND_LOW = -2.5
BAND_SPAN = 5.0
HALF = 64


def from_behind(block, axis, distance):
    devices = range(lax.axis_size(axis))
    route = [(i - distance, i) for i in devices if i - distance in devices]
    return lax.ppermute(block, axis, route)


def dot(x, y):
    return lax.dot_general(x, y, (((1,), (0,)), ((), ())), precision=PRECISE, preferred_element_type=jnp.float32)

def packed_sign(shape):
    li = lax.broadcasted_iota(jnp.int32, shape, 1)
    return jnp.where(li < HALF, -1.0, 1.0)

def rot(x):
    return pltpu.roll(x, HALF, 1) * packed_sign((1, 2 * HALF))

def pprod(x, y):
    return dot(x, jnp.concatenate([y, rot(y)], axis=0))

def leaves(blocks):
    n = HALF // 8
    li = lax.broadcasted_iota(jnp.int32, (8, 2 * HALF), 1)
    si = lax.broadcasted_iota(jnp.int32, (8, 2 * HALF), 0)
    sign = jnp.where(li < HALF, -1.0, 1.0)
    wide = lambda x: jnp.broadcast_to(x, (8, 2 * HALF))
    tiles = [[b[8 * t:8 * t + 8] for t in range(n)] for b in blocks]
    for g in range(n):
        base = 8 * g
        for rows in tiles:
            panel = rows[g]
            spun = pltpu.roll(panel, HALF, 1) * sign
            cr = [wide(panel[:, base + j:base + j + 1]) for j in range(8)]
            ci = [wide(panel[:, HALF + base + j:HALF + base + j + 1]) for j in range(8)]
            for k in range(8):
                pr, pi = wide(cr[k][k:k + 1]), wide(ci[k][k:k + 1])
                d = 1.0 / (pr * pr + pi * pi)
                ir, ii = pr * d, -pi * d
                row = wide(panel[k:k + 1]) + jnp.where(li == base + k, 1.0, 0.0)
                turn = wide(spun[k:k + 1]) + jnp.where(li == HALF + base + k, 1.0, 0.0)
                v = ir * row + ii * turn
                vt = ir * turn - ii * row
                ur, ui = cr[k] - jnp.where(si == k, 1.0, 0.0), ci[k]
                for j in range(k + 1, 8):
                    xr, xi = wide(cr[j][k:k + 1]), wide(ci[j][k:k + 1])
                    wr = ir * xr - ii * xi
                    wi = ir * xi + ii * xr
                    cr[j] = cr[j] - (ur * wr - ui * wi)
                    ci[j] = ci[j] - (ur * wi + ui * wr)
                panel = panel - (ur * v + ui * vt)
                spun = spun - (ur * vt - ui * v)
            full = panel + jnp.where(li == base + si, 1.0, 0.0)
            turned = spun + jnp.where(li == HALF + base + si, 1.0, 0.0)
            fr = [wide(full[j:j + 1]) for j in range(8)]
            ft = [wide(turned[j:j + 1]) for j in range(8)]
            order = [t for t in range(g + 1, n)] + [t for t in range(g)]
            for t in order:
                x = rows[t]
                terms = [wide(x[:, base + j:base + j + 1]) * fr[j] + wide(x[:, HALF + base + j:HALF + base + j + 1]) * ft[j] for j in range(8)]
                while len(terms) > 1:
                    terms = [p + q for p, q in zip(terms[::2], terms[1::2])]
                rows[t] = x - terms[0]
            rows[g] = panel
    return [jnp.concatenate(rows, axis=0) for rows in tiles]

def quads(x):
    re, im = x
    def q(p, c):
        rows = slice(HALF * p, HALF * (p + 1)); cols = slice(HALF * c, HALF * (c + 1))
        return jnp.concatenate([re[rows, cols], im[rows, cols]], axis=1)
    return q(0, 0), q(0, 1), q(1, 0), q(1, 1)

def planes(qs):
    q00, q01, q10, q11 = qs
    re = jnp.concatenate([jnp.concatenate([q00[:, :HALF], q01[:, :HALF]], 1), jnp.concatenate([q10[:, :HALF], q11[:, :HALF]], 1)], 0)
    im = jnp.concatenate([jnp.concatenate([q00[:, HALF:], q01[:, HALF:]], 1), jnp.concatenate([q10[:, HALF:], q11[:, HALF:]], 1)], 0)
    return re, im

def invert_all(mats):
    qs = [quads(m) for m in mats]
    firsts = leaves([q[0] for q in qs])
    ts, ss, us = [], [], []
    for q, f in zip(qs, firsts):
        t = pprod(q[2], f)
        ts.append(t); us.append(pprod(f, q[1]))
        ss.append(q[3] - pprod(t, q[1]))
    seconds = leaves(ss)
    outs = []
    for f, t, u, s in zip(firsts, ts, us, seconds):
        lower = pprod(s, t)
        outs.append(planes((f + pprod(u, lower), -pprod(u, s), -lower, s)))
    return outs

def cprod(x, y):
    xr, xi = x; yr, yi = y
    lhs = jnp.concatenate([xr, xi], axis=1)
    rhs = jnp.concatenate([jnp.concatenate([yr, yi], 1), jnp.concatenate([-yi, yr], 1)], 0)
    out = dot(lhs, rhs)
    n = yr.shape[1]
    return out[:, :n], out[:, n:]

def adj(x):
    return x[0].T, -x[1].T

def add(x, y): return x[0] + y[0], x[1] + y[1]
def sub(x, y): return x[0] - y[0], x[1] - y[1]

def solve(a, v):
    v0, v1, v2 = v
    h0, h1, h2 = adj(v0), adj(v1), adj(v2)
    g0, g3 = invert_all([a[0], a[3]])
    t0 = cprod(g0, v0)
    d1 = sub(a[1], cprod(h0, t0))
    u3 = cprod(g3, h2)
    d2 = sub(a[2], cprod(v2, u3))
    g2, = invert_all([d2])
    w = cprod(g2, h1)
    green1, = invert_all([sub(d1, cprod(v1, w))])
    green2 = add(g2, cprod(w, cprod(green1, cprod(v1, g2))))
    green0 = add(g0, cprod(t0, cprod(green1, cprod(h0, g0))))
    green3 = add(g3, cprod(u3, cprod(green2, cprod(v2, g3))))
    return green0, green1, green2, green3

def comp_kernel(a_ref, v_ref, g_ref):
    a = [(a_ref[c, 0], a_ref[c, 1]) for c in range(4)]
    v = [(v_ref[c, 0], v_ref[c, 1]) for c in range(3)]
    for c, g in enumerate(solve(a, v)):
        g_ref[c, 0] = g[0]
        g_ref[c, 1] = g[1]

def per_device(hamiltonian, coupling, sigma_in, mode_offsets, mode_coupling, energy_owner):
    slot_count = sigma_in.shape[1]
    orbitals = hamiltonian.shape[-1]
    chain_length = lax.axis_size("cell")
    energy_devices = lax.axis_size("energy")
    chain_index = lax.axis_index("cell")
    energy_index = lax.axis_index("energy")
    energy_count = slot_count * energy_devices
    identity = jnp.eye(orbitals, dtype=jnp.float32)
    at_start = (chain_index == 0).astype(jnp.float32)
    at_end = (chain_index == chain_length - 1).astype(jnp.float32)
    my_owner = lax.dynamic_slice_in_dim(energy_owner, energy_index * slot_count, slot_count)
    energy_level = BAND_LOW + BAND_SPAN * my_owner.astype(jnp.float32) / (energy_count - 1)
    last_r, last_i = coupling[0, 0], coupling[0, 1]
    mm = lambda x, y: jnp.matmul(x, y.T, precision=PRECISE)
    beyond_r = mm(last_r, last_r) + mm(last_i, last_i)
    beyond_i = mm(last_i, last_r) - mm(last_r, last_i)
    fold_r = -LEAD_WIDTH * at_end * beyond_i
    fold_i = LEAD_WIDTH * at_end * beyond_r + (BROADENING + CONTACT_RATE * at_start) * identity
    fold = jnp.stack([fold_r, fold_i])
    level = energy_level[:, None, None, None] * jnp.stack([identity, jnp.zeros_like(identity)])[None]
    block = level + fold[None] - hamiltonian - sigma_in[0]
    mine = lax.all_to_all(block, "cell", 0, 0)
    links = lax.all_gather(coupling[0], "cell")
    green = pl.pallas_call(
        comp_kernel, out_shape=jax.ShapeDtypeStruct(mine.shape, jnp.float32)
    )(mine, links)
    green_diag = lax.all_to_all(green, "cell", 0, 0)[None]

    def weight_rows(source_owner):
        offset_table = source_owner[None, :] - my_owner[:, None]
        matches = (offset_table[:, :, None] == -mode_offsets).astype(jnp.float32) + (
            offset_table[:, :, None] == mode_offsets
        ).astype(jnp.float32)
        return jnp.sum(matches * mode_coupling, -1)

    def contribute(running_sum, blocks, device_offset):
        first_slot = jnp.clip(
            (energy_index - device_offset) * slot_count, 0, energy_count - slot_count
        )
        source_owner = lax.dynamic_slice_in_dim(energy_owner, first_slot, slot_count)
        weights = weight_rows(source_owner)
        return running_sum + jnp.einsum("sk,ckrij->csrij", weights, blocks, precision=PRECISE)

    reach = min(-(-OFFSET_MAX // slot_count), energy_devices - 1)
    sigma_out = contribute(jnp.zeros_like(green_diag), green_diag, 0)
    for distance in range(1, reach + 1):
        for direction in (1, -1):
            arrived = from_behind(green_diag, "energy", direction * distance)
            sigma_out = contribute(sigma_out, arrived, direction * distance)
    return (green_diag, sigma_out)


def solution(mesh):
    in_specs = (
        P("cell", None, None, None),
        P("cell", None, None, None),
        P("cell", "energy", None, None, None),
        P(),
        P(),
        P(),
    )
    out_specs = (P("cell", "energy", None, None, None), P("cell", "energy", None, None, None))
    return jax.shard_map(
        per_device, mesh=mesh, in_specs=in_specs, out_specs=out_specs, check_vma=False
    )
```

```python
import jax
import jax.numpy as jnp
from jax import lax
from jax.experimental import pallas as pl
from jax.experimental.pallas import tpu as pltpu
from jax.sharding import PartitionSpec as P

OFFSET_MAX = 8

PRECISE = lax.Precision.HIGHEST
BROADENING = 0.2
CONTACT_RATE = 0.5
LEAD_WIDTH = 1.0
BAND_LOW = -2.5
BAND_SPAN = 5.0
HALF = 64


def dot(x, y):
    return lax.dot_general(x, y, (((1,), (0,)), ((), ())), precision=PRECISE, preferred_element_type=jnp.float32)

def packed_sign(shape):
    li = lax.broadcasted_iota(jnp.int32, shape, 1)
    return jnp.where(li < HALF, -1.0, 1.0)

def rot(x):
    return pltpu.roll(x, HALF, 1) * packed_sign((1, 2 * HALF))

def pprod(x, y):
    return dot(x, jnp.concatenate([y, rot(y)], axis=0))

def leaves(blocks):
    n = HALF // 8
    li = lax.broadcasted_iota(jnp.int32, (8, 2 * HALF), 1)
    si = lax.broadcasted_iota(jnp.int32, (8, 2 * HALF), 0)
    sign = jnp.where(li < HALF, -1.0, 1.0)
    wide = lambda x: jnp.broadcast_to(x, (8, 2 * HALF))
    tiles = [[b[8 * t:8 * t + 8] for t in range(n)] for b in blocks]
    for g in range(n):
        base = 8 * g
        for rows in tiles:
            panel = rows[g]
            spun = pltpu.roll(panel, HALF, 1) * sign
            cr = [wide(panel[:, base + j:base + j + 1]) for j in range(8)]
            ci = [wide(panel[:, HALF + base + j:HALF + base + j + 1]) for j in range(8)]
            for k in range(8):
                pr, pi = wide(cr[k][k:k + 1]), wide(ci[k][k:k + 1])
                d = 1.0 / (pr * pr + pi * pi)
                ir, ii = pr * d, -pi * d
                row = wide(panel[k:k + 1]) + jnp.where(li == base + k, 1.0, 0.0)
                turn = wide(spun[k:k + 1]) + jnp.where(li == HALF + base + k, 1.0, 0.0)
                v = ir * row + ii * turn
                vt = ir * turn - ii * row
                ur, ui = cr[k] - jnp.where(si == k, 1.0, 0.0), ci[k]
                for j in range(k + 1, 8):
                    xr, xi = wide(cr[j][k:k + 1]), wide(ci[j][k:k + 1])
                    wr = ir * xr - ii * xi
                    wi = ir * xi + ii * xr
                    cr[j] = cr[j] - (ur * wr - ui * wi)
                    ci[j] = ci[j] - (ur * wi + ui * wr)
                panel = panel - (ur * v + ui * vt)
                spun = spun - (ur * vt - ui * v)
            full = panel + jnp.where(li == base + si, 1.0, 0.0)
            turned = spun + jnp.where(li == HALF + base + si, 1.0, 0.0)
            fr = [wide(full[j:j + 1]) for j in range(8)]
            ft = [wide(turned[j:j + 1]) for j in range(8)]
            order = [t for t in range(g + 1, n)] + [t for t in range(g)]
            for t in order:
                x = rows[t]
                terms = [wide(x[:, base + j:base + j + 1]) * fr[j] + wide(x[:, HALF + base + j:HALF + base + j + 1]) * ft[j] for j in range(8)]
                while len(terms) > 1:
                    terms = [p + q for p, q in zip(terms[::2], terms[1::2])]
                rows[t] = x - terms[0]
            rows[g] = panel
    return [jnp.concatenate(rows, axis=0) for rows in tiles]

def quads(x):
    re, im = x
    def q(p, c):
        rows = slice(HALF * p, HALF * (p + 1)); cols = slice(HALF * c, HALF * (c + 1))
        return jnp.concatenate([re[rows, cols], im[rows, cols]], axis=1)
    return q(0, 0), q(0, 1), q(1, 0), q(1, 1)

def planes(qs):
    q00, q01, q10, q11 = qs
    re = jnp.concatenate([jnp.concatenate([q00[:, :HALF], q01[:, :HALF]], 1), jnp.concatenate([q10[:, :HALF], q11[:, :HALF]], 1)], 0)
    im = jnp.concatenate([jnp.concatenate([q00[:, HALF:], q01[:, HALF:]], 1), jnp.concatenate([q10[:, HALF:], q11[:, HALF:]], 1)], 0)
    return re, im

def invert_all(mats):
    qs = [quads(m) for m in mats]
    firsts = leaves([q[0] for q in qs])
    ts, ss, us = [], [], []
    for q, f in zip(qs, firsts):
        t = pprod(q[2], f)
        ts.append(t); us.append(pprod(f, q[1]))
        ss.append(q[3] - pprod(t, q[1]))
    seconds = leaves(ss)
    outs = []
    for f, t, u, s in zip(firsts, ts, us, seconds):
        lower = pprod(s, t)
        outs.append(planes((f + pprod(u, lower), -pprod(u, s), -lower, s)))
    return outs

def cprod(x, y):
    xr, xi = x; yr, yi = y
    lhs = jnp.concatenate([xr, xi], axis=1)
    rhs = jnp.concatenate([jnp.concatenate([yr, yi], 1), jnp.concatenate([-yi, yr], 1)], 0)
    out = dot(lhs, rhs)
    n = yr.shape[1]
    return out[:, :n], out[:, n:]

def adj(x):
    return x[0].T, -x[1].T

def add(x, y): return x[0] + y[0], x[1] + y[1]
def sub(x, y): return x[0] - y[0], x[1] - y[1]

def solve(a, v):
    v0, v1, v2 = v
    h0, h1, h2 = adj(v0), adj(v1), adj(v2)
    g0, g3 = invert_all([a[0], a[3]])
    t0 = cprod(g0, v0)
    d1 = sub(a[1], cprod(h0, t0))
    u3 = cprod(g3, h2)
    d2 = sub(a[2], cprod(v2, u3))
    g2, = invert_all([d2])
    w = cprod(g2, h1)
    green1, = invert_all([sub(d1, cprod(v1, w))])
    green2 = add(g2, cprod(w, cprod(green1, cprod(v1, g2))))
    green0 = add(g0, cprod(t0, cprod(green1, cprod(h0, g0))))
    green3 = add(g3, cprod(u3, cprod(green2, cprod(v2, g3))))
    return green0, green1, green2, green3

def comp_kernel(a_ref, v_ref, g_ref):
    a = [(a_ref[c, 0], a_ref[c, 1]) for c in range(4)]
    v = [(v_ref[c, 0], v_ref[c, 1]) for c in range(3)]
    for c, g in enumerate(solve(a, v)):
        g_ref[c, 0] = g[0]
        g_ref[c, 1] = g[1]

MESH = pl.DeviceIdType.MESH
ARRIVALS = (1, 3, 2)


def remote(source, target, sent, landed, where):
    return pltpu.make_async_remote_copy(
        src_ref=source, dst_ref=target, send_sem=sent, recv_sem=landed,
        device_id=where, device_id_type=MESH,
    )


def gather_kernel(block_ref, link_ref, mine_ref, links_ref, a_sent, a_landed, v_sent, v_landed):
    cells = 4
    me = lax.axis_index("cell")
    other = lambda distance: lax.rem(me + distance, cells)
    barrier = pltpu.get_barrier_semaphore()
    for distance in ARRIVALS:
        pl.semaphore_signal(barrier, 1, device_id={"cell": other(distance)}, device_id_type=MESH)
    pl.semaphore_wait(barrier, cells - 1)

    def a_copy(distance, owner):
        return remote(block_ref.at[other(distance)], mine_ref.at[owner], a_sent.at[distance - 1],
                      a_landed.at[owner], {"cell": other(distance)})

    def v_copy(distance, owner):
        return remote(link_ref.at[0], links_ref.at[owner], v_sent.at[distance - 1],
                      v_landed.at[owner], {"cell": other(distance)})

    for distance in ARRIVALS:
        a_copy(distance, me).start()

    @pl.when(me < cells - 1)
    def _():
        for distance in ARRIVALS:
            v_copy(distance, me).start()
        links_ref[me] = link_ref[0]

    mine_ref[me] = block_ref[me]
    for distance in ARRIVALS:
        a_copy(distance, other(cells - distance)).wait_recv()

        @pl.when(other(cells - distance) < cells - 1)
        def _():
            v_copy(distance, other(cells - distance)).wait_recv()
    for distance in ARRIVALS:
        a_copy(distance, me).wait_send()

    @pl.when(me < cells - 1)
    def _():
        for distance in ARRIVALS:
            v_copy(distance, me).wait_send()


def spread_kernel(weights_ref, green_ref, diag_ref, sigma_ref, near, x_sent, x_landed, z_sent, f_sent, landed):
    cells = 4
    me = lax.axis_index("cell")
    energy = lax.axis_index("energy")
    energies = lax.axis_size("energy")
    core = lax.rem(energy, 2)
    partner = energy + 1 - 2 * core
    lower, upper = energy >= 2, energy < energies - 2
    other = lambda distance: lax.rem(me + distance, cells)
    barrier = pltpu.get_barrier_semaphore()

    def greet(where):
        pl.semaphore_signal(barrier, 1, device_id=where, device_id_type=MESH)

    for distance in ARRIVALS:
        greet({"cell": other(distance)})
    greet({"energy": partner})

    @pl.when(lower)
    def _():
        greet({"energy": energy - 2})

    @pl.when(upper)
    def _():
        greet({"energy": energy + 2})
    pl.semaphore_wait(barrier, cells + lower.astype(jnp.int32) + upper.astype(jnp.int32))

    def x_copy(distance, slot):
        return remote(green_ref.at[other(distance)], diag_ref.at[slot], x_sent.at[distance - 1],
                      x_landed.at[slot], {"cell": other(distance)})

    def from_slot(step):
        return me if step == 0 else other(cells - ARRIVALS[step - 1])

    def source(step):
        return green_ref.at[me] if step == 0 else diag_ref.at[from_slot(step)]

    def up(step):
        slot = from_slot(step)
        return remote(source(step), near.at[0, slot], z_sent.at[0, step], landed.at[0, slot], {"energy": energy + 2})

    def down(step):
        slot = from_slot(step)
        return remote(source(step), near.at[3, slot], z_sent.at[1, step], landed.at[3, slot], {"energy": energy - 2})

    def across(step):
        slot = from_slot(step)
        return remote(source(step), near.at[1 + core, slot], z_sent.at[2, step], landed.at[1 + core, slot], {"energy": partner})

    def forward(step, sees, place):
        slot = from_slot(step)
        return remote(near.at[sees, slot], near.at[place, slot], f_sent.at[step], landed.at[place, slot], {"energy": partner})

    def arrived(side, step):
        slot = from_slot(step)
        remote(near.at[side, slot], near.at[side, slot], f_sent.at[step], landed.at[side, slot], {"energy": partner}).wait_recv()

    for distance in ARRIVALS:
        x_copy(distance, me).start()

    def send(step):
        @pl.when(upper)
        def _():
            up(step).start()

        @pl.when(lower)
        def _():
            down(step).start()
        across(step).start()

    def receive_x(step):
        distance = ARRIVALS[step - 1]
        x_copy(distance, other(cells - distance)).wait_recv()
        send(step)

    def relay(step):
        @pl.when(lower)
        def _():
            arrived(0, step)

            @pl.when(core == 1)
            def _():
                forward(step, 0, 1).start()

        @pl.when(upper)
        def _():
            arrived(3, step)

            @pl.when(core == 0)
            def _():
                forward(step, 3, 2).start()

    def finish(step):
        @pl.when(jnp.logical_or(core == 1, lower))
        def _():
            arrived(1, step)

        @pl.when(jnp.logical_or(core == 0, upper))
        def _():
            arrived(2, step)
        slot = from_slot(step)
        blocks = [near[0, slot], near[1, slot], diag_ref[slot], near[2, slot], near[3, slot]]
        for q in range(4):
            total = weights_ref[q, slot] * blocks[0]
            for o in range(1, 5):
                total += weights_ref[q, 4 * o + slot] * blocks[o]
            sigma_ref[q] = total if step == 0 else sigma_ref[q] + total

    send(0)
    diag_ref[me] = green_ref[me]
    zero = jnp.zeros(near.shape[1:], jnp.float32)

    @pl.when(jnp.logical_not(lower))
    def _():
        near[0] = zero

        @pl.when(core == 0)
        def _():
            near[1] = zero

    @pl.when(jnp.logical_not(upper))
    def _():
        near[3] = zero

        @pl.when(core == 1)
        def _():
            near[2] = zero
    receive_x(1)
    receive_x(2)
    relay(0)
    receive_x(3)
    relay(1)
    finish(0)
    relay(2)
    finish(1)
    relay(3)
    finish(2)
    finish(3)
    for distance in ARRIVALS:
        x_copy(distance, me).wait_send()
    for step in range(4):
        @pl.when(upper)
        def _():
            up(step).wait_send()

        @pl.when(lower)
        def _():
            down(step).wait_send()
        across(step).wait_send()

        @pl.when(jnp.logical_and(core == 1, lower))
        def _():
            forward(step, 0, 1).wait_send()

        @pl.when(jnp.logical_and(core == 0, upper))
        def _():
            forward(step, 3, 2).wait_send()


def gather(block, links):
    vmem = pl.BlockSpec(memory_space=pltpu.VMEM)
    dma = pltpu.SemaphoreType.DMA
    return pl.pallas_call(
        gather_kernel,
        out_shape=(
            jax.ShapeDtypeStruct(block.shape, jnp.float32),
            jax.ShapeDtypeStruct((3,) + block.shape[1:], jnp.float32),
        ),
        in_specs=[vmem, vmem],
        out_specs=(vmem, vmem),
        scratch_shapes=[dma((3,)), dma((4,)), dma((3,)), dma((3,))],
        compiler_params=pltpu.CompilerParams(collective_id=0, has_side_effects=True),
    )(block, links)


def spread(weights, green):
    vmem = pl.BlockSpec(memory_space=pltpu.VMEM)
    dma = pltpu.SemaphoreType.DMA
    shape = jax.ShapeDtypeStruct(green.shape, jnp.float32)
    return pl.pallas_call(
        spread_kernel,
        out_shape=(shape, shape),
        in_specs=[pl.BlockSpec(memory_space=pltpu.SMEM), vmem],
        out_specs=(vmem, vmem),
        scratch_shapes=[
            pltpu.VMEM((4,) + green.shape, jnp.float32),
            dma((3,)), dma((4,)), dma((3, 4)), dma((4,)), dma((4, 4)),
        ],
        compiler_params=pltpu.CompilerParams(collective_id=1, has_side_effects=True),
    )(weights, green)


def per_device(hamiltonian, coupling, sigma_in, mode_offsets, mode_coupling, energy_owner):
    slot_count = sigma_in.shape[1]
    orbitals = hamiltonian.shape[-1]
    chain_length = lax.axis_size("cell")
    energy_devices = lax.axis_size("energy")
    chain_index = lax.axis_index("cell")
    energy_index = lax.axis_index("energy")
    energy_count = slot_count * energy_devices
    identity = jnp.eye(orbitals, dtype=jnp.float32)
    at_start = (chain_index == 0).astype(jnp.float32)
    at_end = (chain_index == chain_length - 1).astype(jnp.float32)
    my_owner = lax.dynamic_slice_in_dim(energy_owner, energy_index * slot_count, slot_count)
    energy_level = BAND_LOW + BAND_SPAN * my_owner.astype(jnp.float32) / (energy_count - 1)
    last_r, last_i = coupling[0, 0], coupling[0, 1]
    mm = lambda x, y: jnp.matmul(x, y.T, precision=PRECISE)
    beyond_r = mm(last_r, last_r) + mm(last_i, last_i)
    beyond_i = mm(last_i, last_r) - mm(last_r, last_i)
    fold_r = -LEAD_WIDTH * at_end * beyond_i
    fold_i = LEAD_WIDTH * at_end * beyond_r + (BROADENING + CONTACT_RATE * at_start) * identity
    fold = jnp.stack([fold_r, fold_i])
    level = energy_level[:, None, None, None] * jnp.stack([identity, jnp.zeros_like(identity)])[None]
    block = level + fold[None] - hamiltonian - sigma_in[0]
    mine, links = gather(block, coupling)
    green = pl.pallas_call(
        comp_kernel, out_shape=jax.ShapeDtypeStruct(mine.shape, jnp.float32)
    )(mine, links)
    padded = jnp.pad(energy_owner, OFFSET_MAX, constant_values=-4 * energy_count)
    window = lax.dynamic_slice_in_dim(padded, energy_index * slot_count, slot_count + 2 * OFFSET_MAX)
    apart = (window[None, :] - my_owner[:, None])[:, :, None]
    matches = (apart == -mode_offsets).astype(jnp.float32) + (apart == mode_offsets).astype(jnp.float32)
    green_diag, sigma_out = spread(jnp.sum(matches * mode_coupling, -1), green)
    return (green_diag[None], sigma_out[None])


def solution(mesh):
    in_specs = (
        P("cell", None, None, None),
        P("cell", None, None, None),
        P("cell", "energy", None, None, None),
        P(),
        P(),
        P(),
    )
    out_specs = (P("cell", "energy", None, None, None), P("cell", "energy", None, None, None))
    return jax.shard_map(
        per_device, mesh=mesh, in_specs=in_specs, out_specs=out_specs, check_vma=False
    )
```

```python
import jax
import jax.numpy as jnp
from jax import lax
from jax.experimental import pallas as pl
from jax.experimental.pallas import tpu as pltpu
from jax.sharding import PartitionSpec as P

OFFSET_MAX = 8

PRECISE = lax.Precision.HIGHEST
BROADENING = 0.2
CONTACT_RATE = 0.5
LEAD_WIDTH = 1.0
BAND_LOW = -2.5
BAND_SPAN = 5.0
HALF = 64


def dot(x, y):
    return lax.dot_general(x, y, (((1,), (0,)), ((), ())), precision=PRECISE, preferred_element_type=jnp.float32)

def packed_sign(shape):
    li = lax.broadcasted_iota(jnp.int32, shape, 1)
    return jnp.where(li < HALF, -1.0, 1.0)

def rot(x):
    return pltpu.roll(x, HALF, 1) * packed_sign((1, 2 * HALF))

def pprod(x, y):
    return dot(x, jnp.concatenate([y, rot(y)], axis=0))

def leaves(blocks):
    n = HALF // 8
    li = lax.broadcasted_iota(jnp.int32, (8, 2 * HALF), 1)
    si = lax.broadcasted_iota(jnp.int32, (8, 2 * HALF), 0)
    sign = jnp.where(li < HALF, -1.0, 1.0)
    wide = lambda x: jnp.broadcast_to(x, (8, 2 * HALF))
    tiles = [[b[8 * t:8 * t + 8] for t in range(n)] for b in blocks]
    for g in range(n):
        base = 8 * g
        for rows in tiles:
            panel = rows[g]
            spun = pltpu.roll(panel, HALF, 1) * sign
            cr = [wide(panel[:, base + j:base + j + 1]) for j in range(8)]
            ci = [wide(panel[:, HALF + base + j:HALF + base + j + 1]) for j in range(8)]
            for k in range(8):
                pr, pi = wide(cr[k][k:k + 1]), wide(ci[k][k:k + 1])
                d = 1.0 / (pr * pr + pi * pi)
                ir, ii = pr * d, -pi * d
                row = wide(panel[k:k + 1]) + jnp.where(li == base + k, 1.0, 0.0)
                turn = wide(spun[k:k + 1]) + jnp.where(li == HALF + base + k, 1.0, 0.0)
                v = ir * row + ii * turn
                vt = ir * turn - ii * row
                ur, ui = cr[k] - jnp.where(si == k, 1.0, 0.0), ci[k]
                for j in range(k + 1, 8):
                    xr, xi = wide(cr[j][k:k + 1]), wide(ci[j][k:k + 1])
                    wr = ir * xr - ii * xi
                    wi = ir * xi + ii * xr
                    cr[j] = cr[j] - (ur * wr - ui * wi)
                    ci[j] = ci[j] - (ur * wi + ui * wr)
                panel = panel - (ur * v + ui * vt)
                spun = spun - (ur * vt - ui * v)
            full = panel + jnp.where(li == base + si, 1.0, 0.0)
            turned = spun + jnp.where(li == HALF + base + si, 1.0, 0.0)
            fr = [wide(full[j:j + 1]) for j in range(8)]
            ft = [wide(turned[j:j + 1]) for j in range(8)]
            order = [t for t in range(g + 1, n)] + [t for t in range(g)]
            for t in order:
                x = rows[t]
                terms = [wide(x[:, base + j:base + j + 1]) * fr[j] + wide(x[:, HALF + base + j:HALF + base + j + 1]) * ft[j] for j in range(8)]
                while len(terms) > 1:
                    terms = [p + q for p, q in zip(terms[::2], terms[1::2])]
                rows[t] = x - terms[0]
            rows[g] = panel
    return [jnp.concatenate(rows, axis=0) for rows in tiles]

def quads(x):
    re, im = x
    def q(p, c):
        rows = slice(HALF * p, HALF * (p + 1)); cols = slice(HALF * c, HALF * (c + 1))
        return jnp.concatenate([re[rows, cols], im[rows, cols]], axis=1)
    return q(0, 0), q(0, 1), q(1, 0), q(1, 1)

def planes(qs):
    q00, q01, q10, q11 = qs
    re = jnp.concatenate([jnp.concatenate([q00[:, :HALF], q01[:, :HALF]], 1), jnp.concatenate([q10[:, :HALF], q11[:, :HALF]], 1)], 0)
    im = jnp.concatenate([jnp.concatenate([q00[:, HALF:], q01[:, HALF:]], 1), jnp.concatenate([q10[:, HALF:], q11[:, HALF:]], 1)], 0)
    return re, im

def invert_all(mats):
    qs = [quads(m) for m in mats]
    firsts = leaves([q[0] for q in qs])
    ts, ss, us = [], [], []
    for q, f in zip(qs, firsts):
        t = pprod(q[2], f)
        ts.append(t); us.append(pprod(f, q[1]))
        ss.append(q[3] - pprod(t, q[1]))
    seconds = leaves(ss)
    outs = []
    for f, t, u, s in zip(firsts, ts, us, seconds):
        lower = pprod(s, t)
        outs.append(planes((f + pprod(u, lower), -pprod(u, s), -lower, s)))
    return outs

def cprod(x, y):
    xr, xi = x; yr, yi = y
    lhs = jnp.concatenate([xr, xi], axis=1)
    rhs = jnp.concatenate([jnp.concatenate([yr, yi], 1), jnp.concatenate([-yi, yr], 1)], 0)
    out = dot(lhs, rhs)
    n = yr.shape[1]
    return out[:, :n], out[:, n:]

def adj(x):
    return x[0].T, -x[1].T

def add(x, y): return x[0] + y[0], x[1] + y[1]
def sub(x, y): return x[0] - y[0], x[1] - y[1]

def solve(block, link, keep):
    g0, g3 = invert_all([block(0), block(3)])
    v0, v2 = link(0), link(2)
    h0, h2 = adj(v0), adj(v2)
    t0 = cprod(g0, v0)
    u3 = cprod(g3, h2)
    d2 = sub(block(2), cprod(v2, u3))
    g2, = invert_all([d2])
    d1 = sub(block(1), cprod(h0, t0))
    v1 = link(1)
    w = cprod(g2, adj(v1))
    green1, = invert_all([sub(d1, cprod(v1, w))])
    keep(1, green1)
    green2 = add(g2, cprod(w, cprod(green1, cprod(v1, g2))))
    keep(2, green2)
    keep(0, add(g0, cprod(t0, cprod(green1, cprod(h0, g0)))))
    keep(3, add(g3, cprod(u3, cprod(green2, cprod(v2, g3)))))


MESH = pl.DeviceIdType.MESH
ARRIVALS = (1, 3, 2)


def remote(source, target, sent, landed, where):
    return pltpu.make_async_remote_copy(
        src_ref=source, dst_ref=target, send_sem=sent, recv_sem=landed,
        device_id=where, device_id_type=MESH,
    )


def chain_kernel(owner_ref, ham_ref, link_ref, self_ref, green_ref, sends, mine, links, fold,
                 a_sent, a_landed, v_sent, v_landed):
    cells, slots = 4, 4
    me = lax.axis_index("cell")
    energy = lax.axis_index("energy")
    last = slots * lax.axis_size("energy") - 1
    other = lambda distance: lax.rem(me + distance, cells)
    barrier = pltpu.get_barrier_semaphore()
    for distance in ARRIVALS:
        pl.semaphore_signal(barrier, 1, device_id={"cell": other(distance)}, device_id_type=MESH)
    side = fold.shape[-1]
    eye = jnp.where(
        lax.broadcasted_iota(jnp.int32, (side, side), 0) == lax.broadcasted_iota(jnp.int32, (side, side), 1), 1.0, 0.0)
    at_start = jnp.where(me == 0, CONTACT_RATE, 0.0)
    fold[0] = -ham_ref[0, 0]
    fold[1] = (BROADENING + at_start) * eye - ham_ref[0, 1]

    @pl.when(me == cells - 1)
    def _():
        link = link_ref[0, 0], link_ref[0, 1]
        beyond = cprod(link, adj(link))
        fold[0] = fold[0] - LEAD_WIDTH * beyond[1]
        fold[1] = fold[1] + LEAD_WIDTH * beyond[0]

    def make(slot, target, at):
        index = jnp.full((1, side), owner_ref[slots * energy + slot], jnp.int32)
        level = BAND_LOW + BAND_SPAN * index.astype(jnp.float32) / last
        target[at, 0] = level * eye + fold[0] - self_ref[0, slot, 0]
        target[at, 1] = fold[1] - self_ref[0, slot, 1]

    for distance in ARRIVALS:
        make(other(distance), sends, distance - 1)
    make(me, mine, me)
    pl.semaphore_wait(barrier, cells - 1)

    def a_copy(distance, owner):
        return remote(sends.at[distance - 1], mine.at[owner], a_sent.at[distance - 1],
                      a_landed.at[owner], {"cell": other(distance)})

    def v_copy(distance, owner):
        return remote(link_ref.at[0], links.at[owner], v_sent.at[distance - 1],
                      v_landed.at[owner], {"cell": other(distance)})

    for distance in ARRIVALS:
        a_copy(distance, me).start()

    @pl.when(me < cells - 1)
    def _():
        for distance in ARRIVALS:
            v_copy(distance, me).start()
        links[me] = link_ref[0]

    def wait_a(cell):
        @pl.when(me != cell)
        def _():
            a_copy(1, cell).wait_recv()
        return mine[cell, 0], mine[cell, 1]

    def wait_v(cell):
        @pl.when(me != cell)
        def _():
            v_copy(1, cell).wait_recv()
        return links[cell, 0], links[cell, 1]

    def keep(cell, green):
        green_ref[cell, 0] = green[0]
        green_ref[cell, 1] = green[1]

    solve(wait_a, wait_v, keep)
    for distance in ARRIVALS:
        a_copy(distance, me).wait_send()

    @pl.when(me < cells - 1)
    def _():
        for distance in ARRIVALS:
            v_copy(distance, me).wait_send()


def spread_kernel(owner_ref, offsets_ref, strengths_ref, green_ref, diag_ref, sigma_ref, near, weights, x_sent, x_landed, z_sent, f_sent, landed):
    cells = 4
    me = lax.axis_index("cell")
    energy = lax.axis_index("energy")
    energies = lax.axis_size("energy")
    core = lax.rem(energy, 2)
    partner = energy + 1 - 2 * core
    lower, upper = energy >= 2, energy < energies - 2
    other = lambda distance: lax.rem(me + distance, cells)
    barrier = pltpu.get_barrier_semaphore()

    def greet(where):
        pl.semaphore_signal(barrier, 1, device_id=where, device_id_type=MESH)

    for distance in ARRIVALS:
        greet({"cell": other(distance)})
    greet({"energy": partner})

    @pl.when(lower)
    def _():
        greet({"energy": energy - 2})

    @pl.when(upper)
    def _():
        greet({"energy": energy + 2})
    pl.semaphore_wait(barrier, cells + lower.astype(jnp.int32) + upper.astype(jnp.int32))

    def x_copy(distance, slot):
        return remote(green_ref.at[other(distance)], diag_ref.at[slot], x_sent.at[distance - 1],
                      x_landed.at[slot], {"cell": other(distance)})

    def from_slot(step):
        return me if step == 0 else other(cells - ARRIVALS[step - 1])

    def source(step):
        return green_ref.at[me] if step == 0 else diag_ref.at[from_slot(step)]

    def up(step):
        slot = from_slot(step)
        return remote(source(step), near.at[0, slot], z_sent.at[0, step], landed.at[0, slot], {"energy": energy + 2})

    def down(step):
        slot = from_slot(step)
        return remote(source(step), near.at[3, slot], z_sent.at[1, step], landed.at[3, slot], {"energy": energy - 2})

    def across(step):
        slot = from_slot(step)
        return remote(source(step), near.at[1 + core, slot], z_sent.at[2, step], landed.at[1 + core, slot], {"energy": partner})

    def forward(step, sees, place):
        slot = from_slot(step)
        return remote(near.at[sees, slot], near.at[place, slot], f_sent.at[step], landed.at[place, slot], {"energy": partner})

    def arrived(side, step):
        slot = from_slot(step)
        remote(near.at[side, slot], near.at[side, slot], f_sent.at[step], landed.at[side, slot], {"energy": partner}).wait_recv()

    for distance in ARRIVALS:
        x_copy(distance, me).start()

    def send(step):
        @pl.when(upper)
        def _():
            up(step).start()

        @pl.when(lower)
        def _():
            down(step).start()
        across(step).start()

    def receive_x(step):
        distance = ARRIVALS[step - 1]
        x_copy(distance, other(cells - distance)).wait_recv()
        send(step)

    def relay(step):
        @pl.when(lower)
        def _():
            arrived(0, step)

            @pl.when(core == 1)
            def _():
                forward(step, 0, 1).start()

        @pl.when(upper)
        def _():
            arrived(3, step)

            @pl.when(core == 0)
            def _():
                forward(step, 3, 2).start()

    def finish(step):
        @pl.when(jnp.logical_or(core == 1, lower))
        def _():
            arrived(1, step)

        @pl.when(jnp.logical_or(core == 0, upper))
        def _():
            arrived(2, step)
        slot = from_slot(step)
        blocks = [near[0, slot], near[1, slot], diag_ref[slot], near[2, slot], near[3, slot]]
        for q in range(4):
            total = weights[q, step] * blocks[0]
            for o in range(1, 5):
                total += weights[q, 4 * o + step] * blocks[o]
            sigma_ref[q] = total if step == 0 else sigma_ref[q] + total

    send(0)
    diag_ref[me] = green_ref[me]
    zero = jnp.zeros(near.shape[1:], jnp.float32)

    @pl.when(jnp.logical_not(lower))
    def _():
        near[0] = zero

        @pl.when(core == 0)
        def _():
            near[1] = zero

    @pl.when(jnp.logical_not(upper))
    def _():
        near[3] = zero

        @pl.when(core == 1)
        def _():
            near[2] = zero

    def weigh(q, o, step):
        place = jnp.clip(4 * (energy + o - 2) + from_slot(step), 0, 4 * energies - 1)
        apart = jnp.abs(owner_ref[place] - owner_ref[4 * energy + q])
        terms = [jnp.where(apart == offsets_ref[m], strengths_ref[m], 0.0) for m in range(4)]
        weights[q, 4 * o + step] = (terms[0] + terms[1]) + (terms[2] + terms[3])

    for q in range(4):
        for o in range(5):
            for step in range(4):
                weigh(q, o, step)
    receive_x(1)
    receive_x(2)
    relay(0)
    receive_x(3)
    relay(1)
    finish(0)
    relay(2)
    finish(1)
    relay(3)
    finish(2)
    finish(3)
    for distance in ARRIVALS:
        x_copy(distance, me).wait_send()
    for step in range(4):
        @pl.when(upper)
        def _():
            up(step).wait_send()

        @pl.when(lower)
        def _():
            down(step).wait_send()
        across(step).wait_send()

        @pl.when(jnp.logical_and(core == 1, lower))
        def _():
            forward(step, 0, 1).wait_send()

        @pl.when(jnp.logical_and(core == 0, upper))
        def _():
            forward(step, 3, 2).wait_send()


def chain(owner, hamiltonian, coupling, sigma_in):
    vmem = pl.BlockSpec(memory_space=pltpu.VMEM)
    dma = pltpu.SemaphoreType.DMA
    shape = sigma_in.shape[1:]
    buffer = lambda count: pltpu.VMEM((count,) + shape[1:], jnp.float32)
    return pl.pallas_call(
        chain_kernel,
        out_shape=jax.ShapeDtypeStruct(shape, jnp.float32),
        in_specs=[pl.BlockSpec(memory_space=pltpu.SMEM), vmem, vmem, vmem],
        out_specs=vmem,
        scratch_shapes=[
            buffer(3), buffer(4), buffer(3), pltpu.VMEM(shape[1:], jnp.float32),
            dma((3,)), dma((4,)), dma((3,)), dma((3,)),
        ],
        compiler_params=pltpu.CompilerParams(collective_id=0, has_side_effects=True),
    )(owner, hamiltonian, coupling, sigma_in)


def spread(owner, offsets, strengths, green):
    vmem = pl.BlockSpec(memory_space=pltpu.VMEM)
    dma = pltpu.SemaphoreType.DMA
    shape = jax.ShapeDtypeStruct(green.shape, jnp.float32)
    return pl.pallas_call(
        spread_kernel,
        out_shape=(shape, shape),
        in_specs=[pl.BlockSpec(memory_space=pltpu.SMEM)] * 3 + [vmem],
        out_specs=(vmem, vmem),
        scratch_shapes=[
            pltpu.VMEM((4,) + green.shape, jnp.float32),
            pltpu.SMEM((4, 20), jnp.float32),
            dma((3,)), dma((4,)), dma((3, 4)), dma((4,)), dma((4, 4)),
        ],
        compiler_params=pltpu.CompilerParams(collective_id=1, has_side_effects=True),
    )(owner, offsets, strengths, green)


def per_device(hamiltonian, coupling, sigma_in, mode_offsets, mode_coupling, energy_owner):
    green = chain(energy_owner, hamiltonian, coupling, sigma_in)
    green_diag, sigma_out = spread(energy_owner, mode_offsets, mode_coupling, green)
    return (green_diag[None], sigma_out[None])


def solution(mesh):
    in_specs = (
        P("cell", None, None, None),
        P("cell", None, None, None),
        P("cell", "energy", None, None, None),
        P(),
        P(),
        P(),
    )
    out_specs = (P("cell", "energy", None, None, None), P("cell", "energy", None, None, None))
    return jax.shard_map(
        per_device, mesh=mesh, in_specs=in_specs, out_specs=out_specs, check_vma=False
    )
```

```python
import jax
import jax.numpy as jnp
from jax import lax
from jax.experimental import pallas as pl
from jax.experimental.pallas import tpu as pltpu
from jax.sharding import PartitionSpec as P

OFFSET_MAX = 8

PRECISE = lax.Precision.HIGHEST
BROADENING = 0.2
CONTACT_RATE = 0.5
LEAD_WIDTH = 1.0
BAND_LOW = -2.5
BAND_SPAN = 5.0
HALF = 64
VMEM_LIMIT = 16 * 2**20


def dot(x, y):
    return lax.dot_general(x, y, (((1,), (0,)), ((), ())), precision=PRECISE, preferred_element_type=jnp.float32)

def packed_sign(shape):
    li = lax.broadcasted_iota(jnp.int32, shape, 1)
    return jnp.where(li < HALF, -1.0, 1.0)

def rot(x):
    return pltpu.roll(x, HALF, 1) * packed_sign((1, 2 * HALF))

def pprod(x, y):
    return dot(x, jnp.concatenate([y, rot(y)], axis=0))

def leaves(blocks):
    n = HALF // 8
    li = lax.broadcasted_iota(jnp.int32, (8, 2 * HALF), 1)
    si = lax.broadcasted_iota(jnp.int32, (8, 2 * HALF), 0)
    sign = jnp.where(li < HALF, -1.0, 1.0)
    wide = lambda x: jnp.broadcast_to(x, (8, 2 * HALF))
    tiles = [[b[8 * t:8 * t + 8] for t in range(n)] for b in blocks]
    for g in range(n):
        base = 8 * g
        for rows in tiles:
            panel = rows[g]
            spun = pltpu.roll(panel, HALF, 1) * sign
            cr = [wide(panel[:, base + j:base + j + 1]) for j in range(8)]
            ci = [wide(panel[:, HALF + base + j:HALF + base + j + 1]) for j in range(8)]
            for k in range(8):
                pr, pi = wide(cr[k][k:k + 1]), wide(ci[k][k:k + 1])
                d = 1.0 / (pr * pr + pi * pi)
                ur, ui = cr[k] - jnp.where(si == k, 1.0, 0.0), ci[k]
                for j in range(k + 1, 8):
                    xr, xi = wide(cr[j][k:k + 1]), wide(ci[j][k:k + 1])
                    wr = xr * pr + xi * pi
                    wi = xi * pr - xr * pi
                    cr[j] = cr[j] - d * (ur * wr - ui * wi)
                    ci[j] = ci[j] - d * (ur * wi + ui * wr)
                row = wide(panel[k:k + 1]) + jnp.where(li == base + k, 1.0, 0.0)
                turn = wide(spun[k:k + 1]) + jnp.where(li == HALF + base + k, 1.0, 0.0)
                v = row * pr - turn * pi
                vt = turn * pr + row * pi
                panel = panel - d * (ur * v + ui * vt)
                spun = spun - d * (ur * vt - ui * v)
            full = panel + jnp.where(li == base + si, 1.0, 0.0)
            turned = spun + jnp.where(li == HALF + base + si, 1.0, 0.0)
            fr = [wide(full[j:j + 1]) for j in range(8)]
            ft = [wide(turned[j:j + 1]) for j in range(8)]
            near = [g + 1] if g + 1 < n else []
            far = [t for t in range(g + 2, n)] + [t for t in range(g)]
            for t in near:
                x = rows[t]
                terms = [wide(x[:, base + j:base + j + 1]) * fr[j] + wide(x[:, HALF + base + j:HALF + base + j + 1]) * ft[j] for j in range(8)]
                while len(terms) > 1:
                    terms = [p + q for p, q in zip(terms[::2], terms[1::2])]
                rows[t] = x - terms[0]
            empty = jnp.zeros_like(full)
            weight = jnp.concatenate([full if t == g else turned if t == g + n else empty for t in range(2 * n)], axis=0)
            moved = dot(jnp.concatenate([rows[t] for t in far], axis=0), weight)
            for at, t in enumerate(far):
                rows[t] = rows[t] - moved[8 * at:8 * at + 8]
            rows[g] = panel
    return [jnp.concatenate(rows, axis=0) for rows in tiles]

def quads(x):
    re, im = x
    def q(p, c):
        rows = slice(HALF * p, HALF * (p + 1)); cols = slice(HALF * c, HALF * (c + 1))
        return jnp.concatenate([re[rows, cols], im[rows, cols]], axis=1)
    return q(0, 0), q(0, 1), q(1, 0), q(1, 1)

def planes(qs):
    q00, q01, q10, q11 = qs
    re = jnp.concatenate([jnp.concatenate([q00[:, :HALF], q01[:, :HALF]], 1), jnp.concatenate([q10[:, :HALF], q11[:, :HALF]], 1)], 0)
    im = jnp.concatenate([jnp.concatenate([q00[:, HALF:], q01[:, HALF:]], 1), jnp.concatenate([q10[:, HALF:], q11[:, HALF:]], 1)], 0)
    return re, im

def invert_all(mats):
    qs = [quads(m) for m in mats]
    firsts = leaves([q[0] for q in qs])
    ts, ss, us = [], [], []
    for q, f in zip(qs, firsts):
        t = pprod(q[2], f)
        ts.append(t); us.append(pprod(f, q[1]))
        ss.append(q[3] - pprod(t, q[1]))
    seconds = leaves(ss)
    outs = []
    for f, t, u, s in zip(firsts, ts, us, seconds):
        lower = pprod(s, t)
        outs.append(planes((f + pprod(u, lower), -pprod(u, s), -lower, s)))
    return outs

def cprod(x, y):
    xr, xi = x; yr, yi = y
    lhs = jnp.concatenate([xr, xi], axis=1)
    rhs = jnp.concatenate([jnp.concatenate([yr, yi], 1), jnp.concatenate([-yi, yr], 1)], 0)
    out = dot(lhs, rhs)
    n = yr.shape[1]
    return out[:, :n], out[:, n:]

def adj(x):
    return x[0].T, -x[1].T

def add(x, y): return x[0] + y[0], x[1] + y[1]
def sub(x, y): return x[0] - y[0], x[1] - y[1]

def solve(block, link, keep):
    g0, g3 = invert_all([block(0), block(3)])
    v0, v2 = link(0), link(2)
    h0, h2 = adj(v0), adj(v2)
    t0 = cprod(g0, v0)
    u3 = cprod(g3, h2)
    d2 = sub(block(2), cprod(v2, u3))
    g2, = invert_all([d2])
    d1 = sub(block(1), cprod(h0, t0))
    v1 = link(1)
    w = cprod(g2, adj(v1))
    y2 = cprod(v1, g2)
    y0 = cprod(h0, g0)
    x3 = cprod(v2, g3)
    base3 = add(g3, cprod(u3, cprod(g2, x3)))
    y3 = cprod(y2, x3)
    w3 = cprod(u3, w)
    green1, = invert_all([sub(d1, cprod(v1, w))])
    keep(1, green1)
    keep(2, add(g2, cprod(w, cprod(green1, y2))))
    keep(0, add(g0, cprod(t0, cprod(green1, y0))))
    keep(3, add(base3, cprod(w3, cprod(green1, y3))))


MESH = pl.DeviceIdType.MESH
ARRIVALS = (1, 3, 2)


def remote(source, target, sent, landed, where):
    return pltpu.make_async_remote_copy(
        src_ref=source, dst_ref=target, send_sem=sent, recv_sem=landed,
        device_id=where, device_id_type=MESH,
    )


def chain_kernel(owner_hbm, ham_hbm, link_hbm, self_hbm, green_ref, owner_ref, ham_ref, link_ref, self_ref,
                 sends, mine, links, fold, loaded, a_sent, a_landed, v_sent, v_landed):
    loads = [
        pltpu.make_async_copy(source, target, loaded.at[at])
        for at, (source, target) in enumerate(
            ((owner_hbm, owner_ref), (ham_hbm, ham_ref), (link_hbm, link_ref), (self_hbm, self_ref)))
    ]
    for load in loads:
        load.start()
    cells, slots = 4, 4
    me = lax.axis_index("cell")
    energy = lax.axis_index("energy")
    last = slots * lax.axis_size("energy") - 1
    other = lambda distance: lax.rem(me + distance, cells)
    barrier = pltpu.get_barrier_semaphore()
    for distance in ARRIVALS:
        pl.semaphore_signal(barrier, 1, device_id={"cell": other(distance)}, device_id_type=MESH)
    side = fold.shape[-1]
    eye = jnp.where(
        lax.broadcasted_iota(jnp.int32, (side, side), 0) == lax.broadcasted_iota(jnp.int32, (side, side), 1), 1.0, 0.0)
    at_start = jnp.where(me == 0, CONTACT_RATE, 0.0)
    for load in loads:
        load.wait()
    fold[0] = -ham_ref[0, 0]
    fold[1] = (BROADENING + at_start) * eye - ham_ref[0, 1]

    @pl.when(me == cells - 1)
    def _():
        link = link_ref[0, 0], link_ref[0, 1]
        beyond = cprod(link, adj(link))
        fold[0] = fold[0] - LEAD_WIDTH * beyond[1]
        fold[1] = fold[1] + LEAD_WIDTH * beyond[0]

    def make(slot, target, at):
        index = jnp.full((1, side), owner_ref[slots * energy + slot], jnp.int32)
        level = BAND_LOW + BAND_SPAN * index.astype(jnp.float32) / last
        target[at, 0] = level * eye + fold[0] - self_ref[0, slot, 0]
        target[at, 1] = fold[1] - self_ref[0, slot, 1]

    for distance in ARRIVALS:
        make(other(distance), sends, distance - 1)
    make(me, mine, me)
    pl.semaphore_wait(barrier, cells - 1)

    def a_copy(distance, owner):
        return remote(sends.at[distance - 1], mine.at[owner], a_sent.at[distance - 1],
                      a_landed.at[owner], {"cell": other(distance)})

    def v_copy(distance, owner):
        return remote(link_ref.at[0], links.at[owner], v_sent.at[distance - 1],
                      v_landed.at[owner], {"cell": other(distance)})

    for distance in ARRIVALS:
        a_copy(distance, me).start()

    @pl.when(me < cells - 1)
    def _():
        for distance in ARRIVALS:
            v_copy(distance, me).start()
        links[me] = link_ref[0]

    def wait_a(cell):
        @pl.when(me != cell)
        def _():
            a_copy(1, cell).wait_recv()
        return mine[cell, 0], mine[cell, 1]

    def wait_v(cell):
        @pl.when(me != cell)
        def _():
            v_copy(1, cell).wait_recv()
        return links[cell, 0], links[cell, 1]

    def keep(cell, green):
        green_ref[cell, 0] = green[0]
        green_ref[cell, 1] = green[1]

    solve(wait_a, wait_v, keep)
    for distance in ARRIVALS:
        a_copy(distance, me).wait_send()

    @pl.when(me < cells - 1)
    def _():
        for distance in ARRIVALS:
            v_copy(distance, me).wait_send()


def spread_kernel(owner_ref, offsets_ref, strengths_ref, green_ref, diag_ref, sigma_ref, near, weights, x_sent, x_landed, z_sent, f_sent, landed):
    cells = 4
    me = lax.axis_index("cell")
    energy = lax.axis_index("energy")
    energies = lax.axis_size("energy")
    core = lax.rem(energy, 2)
    partner = energy + 1 - 2 * core
    lower, upper = energy >= 2, energy < energies - 2
    other = lambda distance: lax.rem(me + distance, cells)
    barrier = pltpu.get_barrier_semaphore()

    def greet(where):
        pl.semaphore_signal(barrier, 1, device_id=where, device_id_type=MESH)

    for distance in ARRIVALS:
        greet({"cell": other(distance)})
    greet({"energy": partner})

    @pl.when(lower)
    def _():
        greet({"energy": energy - 2})

    @pl.when(upper)
    def _():
        greet({"energy": energy + 2})
    pl.semaphore_wait(barrier, cells + lower.astype(jnp.int32) + upper.astype(jnp.int32))

    def x_copy(distance, slot):
        return remote(green_ref.at[other(distance)], diag_ref.at[slot], x_sent.at[distance - 1],
                      x_landed.at[slot], {"cell": other(distance)})

    def from_slot(step):
        return me if step == 0 else other(cells - ARRIVALS[step - 1])

    def source(step):
        return green_ref.at[me] if step == 0 else diag_ref.at[from_slot(step)]

    def up(step):
        slot = from_slot(step)
        return remote(source(step), near.at[0, slot], z_sent.at[0, step], landed.at[0, slot], {"energy": energy + 2})

    def down(step):
        slot = from_slot(step)
        return remote(source(step), near.at[3, slot], z_sent.at[1, step], landed.at[3, slot], {"energy": energy - 2})

    def across(step):
        slot = from_slot(step)
        return remote(source(step), near.at[1 + core, slot], z_sent.at[2, step], landed.at[1 + core, slot], {"energy": partner})

    def forward(step, sees, place):
        slot = from_slot(step)
        return remote(near.at[sees, slot], near.at[place, slot], f_sent.at[step], landed.at[place, slot], {"energy": partner})

    def arrived(side, step):
        slot = from_slot(step)
        remote(near.at[side, slot], near.at[side, slot], f_sent.at[step], landed.at[side, slot], {"energy": partner}).wait_recv()

    for distance in ARRIVALS:
        x_copy(distance, me).start()

    def send(step):
        @pl.when(upper)
        def _():
            up(step).start()

        @pl.when(lower)
        def _():
            down(step).start()
        across(step).start()

    def receive_x(step):
        distance = ARRIVALS[step - 1]
        x_copy(distance, other(cells - distance)).wait_recv()
        send(step)

    def relay(step):
        @pl.when(lower)
        def _():
            arrived(0, step)

            @pl.when(core == 1)
            def _():
                forward(step, 0, 1).start()

        @pl.when(upper)
        def _():
            arrived(3, step)

            @pl.when(core == 0)
            def _():
                forward(step, 3, 2).start()

    def finish(step):
        @pl.when(jnp.logical_or(core == 1, lower))
        def _():
            arrived(1, step)

        @pl.when(jnp.logical_or(core == 0, upper))
        def _():
            arrived(2, step)
        slot = from_slot(step)
        blocks = [near[0, slot], near[1, slot], diag_ref[slot], near[2, slot], near[3, slot]]
        for q in range(4):
            total = weights[q, step] * blocks[0]
            for o in range(1, 5):
                total += weights[q, 4 * o + step] * blocks[o]
            sigma_ref[q] = total if step == 0 else sigma_ref[q] + total

    send(0)
    diag_ref[me] = green_ref[me]
    zero = jnp.zeros(near.shape[1:], jnp.float32)

    @pl.when(jnp.logical_not(lower))
    def _():
        near[0] = zero

        @pl.when(core == 0)
        def _():
            near[1] = zero

    @pl.when(jnp.logical_not(upper))
    def _():
        near[3] = zero

        @pl.when(core == 1)
        def _():
            near[2] = zero

    def weigh(q, o, step):
        place = jnp.clip(4 * (energy + o - 2) + from_slot(step), 0, 4 * energies - 1)
        apart = jnp.abs(owner_ref[place] - owner_ref[4 * energy + q])
        terms = [jnp.where(apart == offsets_ref[m], strengths_ref[m], 0.0) for m in range(4)]
        weights[q, 4 * o + step] = (terms[0] + terms[1]) + (terms[2] + terms[3])

    for q in range(4):
        for o in range(5):
            for step in range(4):
                weigh(q, o, step)
    receive_x(1)
    receive_x(2)
    relay(0)
    receive_x(3)
    relay(1)
    finish(0)
    relay(2)
    finish(1)
    relay(3)
    finish(2)
    finish(3)
    for distance in ARRIVALS:
        x_copy(distance, me).wait_send()
    for step in range(4):
        @pl.when(upper)
        def _():
            up(step).wait_send()

        @pl.when(lower)
        def _():
            down(step).wait_send()
        across(step).wait_send()

        @pl.when(jnp.logical_and(core == 1, lower))
        def _():
            forward(step, 0, 1).wait_send()

        @pl.when(jnp.logical_and(core == 0, upper))
        def _():
            forward(step, 3, 2).wait_send()


def chain(owner, hamiltonian, coupling, sigma_in):
    vmem = pl.BlockSpec(memory_space=pltpu.VMEM)
    dma = pltpu.SemaphoreType.DMA
    shape = sigma_in.shape[1:]
    buffer = lambda count: pltpu.VMEM((count,) + shape[1:], jnp.float32)
    return pl.pallas_call(
        chain_kernel,
        out_shape=jax.ShapeDtypeStruct(shape, jnp.float32),
        in_specs=[pl.BlockSpec(memory_space=pltpu.HBM)] * 4,
        out_specs=vmem,
        scratch_shapes=[
            pltpu.SMEM(owner.shape, jnp.int32),
            pltpu.VMEM(hamiltonian.shape, jnp.float32),
            pltpu.VMEM(coupling.shape, jnp.float32),
            pltpu.VMEM(sigma_in.shape, jnp.float32),
            buffer(3), buffer(4), buffer(3), pltpu.VMEM(shape[1:], jnp.float32),
            dma((4,)), dma((3,)), dma((4,)), dma((3,)), dma((3,)),
        ],
        compiler_params=pltpu.CompilerParams(collective_id=0, has_side_effects=True),
    )(owner, hamiltonian, coupling, sigma_in)


def spread(owner, offsets, strengths, green):
    vmem = pl.BlockSpec(memory_space=pltpu.VMEM)
    dma = pltpu.SemaphoreType.DMA
    shape = jax.ShapeDtypeStruct(green.shape, jnp.float32)
    return pl.pallas_call(
        spread_kernel,
        out_shape=(shape, shape),
        in_specs=[pl.BlockSpec(memory_space=pltpu.SMEM)] * 3 + [vmem],
        out_specs=(vmem, vmem),
        scratch_shapes=[
            pltpu.VMEM((4,) + green.shape, jnp.float32),
            pltpu.SMEM((4, 20), jnp.float32),
            dma((3,)), dma((4,)), dma((3, 4)), dma((4,)), dma((4, 4)),
        ],
        compiler_params=pltpu.CompilerParams(collective_id=1, has_side_effects=True, vmem_limit_bytes=VMEM_LIMIT),
    )(owner, offsets, strengths, green)


def write_kernel(diag_ref, sigma_ref, diag_out, sigma_out, done):
    copies = [
        pltpu.make_async_copy(diag_ref, diag_out, done.at[0]),
        pltpu.make_async_copy(sigma_ref, sigma_out, done.at[1]),
    ]
    for copy in copies:
        copy.start()
    for copy in copies:
        copy.wait()


def write(diag, sigma):
    shape = jax.ShapeDtypeStruct(diag.shape, jnp.float32)
    return pl.pallas_call(
        write_kernel,
        out_shape=(shape, shape),
        in_specs=[pl.BlockSpec(memory_space=pltpu.VMEM)] * 2,
        out_specs=(pl.BlockSpec(memory_space=pl.ANY),) * 2,
        scratch_shapes=[pltpu.SemaphoreType.DMA((2,))],
        compiler_params=pltpu.CompilerParams(vmem_limit_bytes=VMEM_LIMIT),
    )(diag, sigma)


def per_device(hamiltonian, coupling, sigma_in, mode_offsets, mode_coupling, energy_owner):
    green = chain(energy_owner, hamiltonian, coupling, sigma_in)
    green_diag, sigma_out = write(*spread(energy_owner, mode_offsets, mode_coupling, green))
    return (green_diag[None], sigma_out[None])


def solution(mesh):
    in_specs = (
        P("cell", None, None, None),
        P("cell", None, None, None),
        P("cell", "energy", None, None, None),
        P(),
        P(),
        P(),
    )
    out_specs = (P("cell", "energy", None, None, None), P("cell", "energy", None, None, None))
    return jax.shard_map(
        per_device, mesh=mesh, in_specs=in_specs, out_specs=out_specs, check_vma=False
    )
```

```python
import jax
import jax.numpy as jnp
from jax import lax
from jax.experimental import pallas as pl
from jax.experimental.pallas import tpu as pltpu
from jax.sharding import PartitionSpec as P

OFFSET_MAX = 8

PRECISE = lax.Precision.HIGHEST
BROADENING = 0.2
CONTACT_RATE = 0.5
LEAD_WIDTH = 1.0
BAND_LOW = -2.5
BAND_SPAN = 5.0
HALF = 64


def dot(x, y):
    return lax.dot_general(x, y, (((1,), (0,)), ((), ())), precision=PRECISE, preferred_element_type=jnp.float32)

def packed_sign(shape):
    li = lax.broadcasted_iota(jnp.int32, shape, 1)
    return jnp.where(li < HALF, -1.0, 1.0)

def rot(x):
    return pltpu.roll(x, HALF, 1) * packed_sign((1, 2 * HALF))

def pprod(x, y):
    return dot(x, jnp.concatenate([y, rot(y)], axis=0))

def leaves(blocks):
    n = HALF // 8
    li = lax.broadcasted_iota(jnp.int32, (8, 2 * HALF), 1)
    si = lax.broadcasted_iota(jnp.int32, (8, 2 * HALF), 0)
    sign = jnp.where(li < HALF, -1.0, 1.0)
    wide = lambda x: jnp.broadcast_to(x, (8, 2 * HALF))
    tiles = [[b[8 * t:8 * t + 8] for t in range(n)] for b in blocks]
    for g in range(n):
        base = 8 * g
        for rows in tiles:
            panel = rows[g]
            spun = pltpu.roll(panel, HALF, 1) * sign
            cr = [wide(panel[:, base + j:base + j + 1]) for j in range(8)]
            ci = [wide(panel[:, HALF + base + j:HALF + base + j + 1]) for j in range(8)]
            for k in range(8):
                pr, pi = wide(cr[k][k:k + 1]), wide(ci[k][k:k + 1])
                d = 1.0 / (pr * pr + pi * pi)
                ur, ui = cr[k] - jnp.where(si == k, 1.0, 0.0), ci[k]
                for j in range(k + 1, 8):
                    xr, xi = wide(cr[j][k:k + 1]), wide(ci[j][k:k + 1])
                    wr = xr * pr + xi * pi
                    wi = xi * pr - xr * pi
                    cr[j] = cr[j] - d * (ur * wr - ui * wi)
                    ci[j] = ci[j] - d * (ur * wi + ui * wr)
                row = wide(panel[k:k + 1]) + jnp.where(li == base + k, 1.0, 0.0)
                turn = wide(spun[k:k + 1]) + jnp.where(li == HALF + base + k, 1.0, 0.0)
                v = row * pr - turn * pi
                vt = turn * pr + row * pi
                panel = panel - d * (ur * v + ui * vt)
                spun = spun - d * (ur * vt - ui * v)
            full = panel + jnp.where(li == base + si, 1.0, 0.0)
            turned = spun + jnp.where(li == HALF + base + si, 1.0, 0.0)
            fr = [wide(full[j:j + 1]) for j in range(8)]
            ft = [wide(turned[j:j + 1]) for j in range(8)]
            near = [g + 1] if g + 1 < n else []
            far = [t for t in range(g + 2, n)] + [t for t in range(g)]
            for t in near:
                x = rows[t]
                terms = [wide(x[:, base + j:base + j + 1]) * fr[j] + wide(x[:, HALF + base + j:HALF + base + j + 1]) * ft[j] for j in range(8)]
                while len(terms) > 1:
                    terms = [p + q for p, q in zip(terms[::2], terms[1::2])]
                rows[t] = x - terms[0]
            empty = jnp.zeros_like(full)
            weight = jnp.concatenate([full if t == g else turned if t == g + n else empty for t in range(2 * n)], axis=0)
            moved = dot(jnp.concatenate([rows[t] for t in far], axis=0), weight)
            for at, t in enumerate(far):
                rows[t] = rows[t] - moved[8 * at:8 * at + 8]
            rows[g] = panel
    return [jnp.concatenate(rows, axis=0) for rows in tiles]

def quads(x):
    re, im = x
    def q(p, c):
        rows = slice(HALF * p, HALF * (p + 1)); cols = slice(HALF * c, HALF * (c + 1))
        return jnp.concatenate([re[rows, cols], im[rows, cols]], axis=1)
    return q(0, 0), q(0, 1), q(1, 0), q(1, 1)

def planes(qs):
    q00, q01, q10, q11 = qs
    re = jnp.concatenate([jnp.concatenate([q00[:, :HALF], q01[:, :HALF]], 1), jnp.concatenate([q10[:, :HALF], q11[:, :HALF]], 1)], 0)
    im = jnp.concatenate([jnp.concatenate([q00[:, HALF:], q01[:, HALF:]], 1), jnp.concatenate([q10[:, HALF:], q11[:, HALF:]], 1)], 0)
    return re, im

def invert_all(mats):
    qs = [quads(m) for m in mats]
    firsts = leaves([q[0] for q in qs])
    ts, ss, us = [], [], []
    for q, f in zip(qs, firsts):
        t = pprod(q[2], f)
        ts.append(t); us.append(pprod(f, q[1]))
        ss.append(q[3] - pprod(t, q[1]))
    seconds = leaves(ss)
    outs = []
    for f, t, u, s in zip(firsts, ts, us, seconds):
        lower = pprod(s, t)
        outs.append(planes((f + pprod(u, lower), -pprod(u, s), -lower, s)))
    return outs

def cprod(x, y):
    xr, xi = x; yr, yi = y
    lhs = jnp.concatenate([xr, xi], axis=1)
    rhs = jnp.concatenate([jnp.concatenate([yr, yi], 1), jnp.concatenate([-yi, yr], 1)], 0)
    out = dot(lhs, rhs)
    n = yr.shape[1]
    return out[:, :n], out[:, n:]

def adj(x):
    return x[0].T, -x[1].T

def add(x, y): return x[0] + y[0], x[1] + y[1]
def sub(x, y): return x[0] - y[0], x[1] - y[1]

def solve(block, link, keep):
    g0, g3 = invert_all([block(0), block(3)])
    v0, v2 = link(0), link(2)
    h0, h2 = adj(v0), adj(v2)
    t0 = cprod(g0, v0)
    u3 = cprod(g3, h2)
    d2 = sub(block(2), cprod(v2, u3))
    g2, = invert_all([d2])
    d1 = sub(block(1), cprod(h0, t0))
    v1 = link(1)
    w = cprod(g2, adj(v1))
    y2 = cprod(v1, g2)
    y0 = cprod(h0, g0)
    x3 = cprod(v2, g3)
    base3 = add(g3, cprod(u3, cprod(g2, x3)))
    y3 = cprod(y2, x3)
    w3 = cprod(u3, w)
    green1, = invert_all([sub(d1, cprod(v1, w))])
    keep(1, green1)
    keep(2, add(g2, cprod(w, cprod(green1, y2))))
    keep(0, add(g0, cprod(t0, cprod(green1, y0))))
    keep(3, add(base3, cprod(w3, cprod(green1, y3))))


MESH = pl.DeviceIdType.MESH
ARRIVALS = (1, 3, 2)


def remote(source, target, sent, landed, where):
    return pltpu.make_async_remote_copy(
        src_ref=source, dst_ref=target, send_sem=sent, recv_sem=landed,
        device_id=where, device_id_type=MESH,
    )


def born_kernel(owner_hbm, ham_hbm, link_hbm, self_hbm, offsets_hbm, strengths_hbm, diag_out, sigma_out,
                diag_ref, sigma_ref, owner_ref, ham_ref, link_ref, self_ref, offsets_ref, strengths_ref, sends, mine, links, fold,
                green_ref, near, weights, loaded, a_sent, a_landed, v_sent, v_landed,
                x_sent, x_landed, z_sent, f_sent, landed, stored):
    loads = [
        pltpu.make_async_copy(source, target, loaded.at[at])
        for at, (source, target) in enumerate(
            ((owner_hbm, owner_ref), (ham_hbm, ham_ref), (link_hbm, link_ref), (self_hbm, self_ref),
             (offsets_hbm, offsets_ref), (strengths_hbm, strengths_ref)))
    ]
    for load in loads:
        load.start()
    cells, slots = 4, 4
    me = lax.axis_index("cell")
    energy = lax.axis_index("energy")
    energies = lax.axis_size("energy")
    last = slots * energies - 1
    core = lax.rem(energy, 2)
    partner = energy + 1 - 2 * core
    lower, upper = energy >= 2, energy < energies - 2
    other = lambda distance: lax.rem(me + distance, cells)
    barrier = pltpu.get_barrier_semaphore()
    def greet(where):
        pl.semaphore_signal(barrier, 1, device_id=where, device_id_type=MESH)

    for distance in ARRIVALS:
        greet({"cell": other(distance)})
    greet({"energy": partner})

    @pl.when(lower)
    def _():
        greet({"energy": energy - 2})

    @pl.when(upper)
    def _():
        greet({"energy": energy + 2})
    side = fold.shape[-1]
    eye = jnp.where(
        lax.broadcasted_iota(jnp.int32, (side, side), 0) == lax.broadcasted_iota(jnp.int32, (side, side), 1), 1.0, 0.0)
    at_start = jnp.where(me == 0, CONTACT_RATE, 0.0)
    for load in loads:
        load.wait()
    fold[0] = -ham_ref[0, 0]
    fold[1] = (BROADENING + at_start) * eye - ham_ref[0, 1]

    @pl.when(me == cells - 1)
    def _():
        link = link_ref[0, 0], link_ref[0, 1]
        beyond = cprod(link, adj(link))
        fold[0] = fold[0] - LEAD_WIDTH * beyond[1]
        fold[1] = fold[1] + LEAD_WIDTH * beyond[0]

    def make(slot, target, at):
        index = jnp.full((1, side), owner_ref[slots * energy + slot], jnp.int32)
        level = BAND_LOW + BAND_SPAN * index.astype(jnp.float32) / last
        target[at, 0] = level * eye + fold[0] - self_ref[0, slot, 0]
        target[at, 1] = fold[1] - self_ref[0, slot, 1]

    for distance in ARRIVALS:
        make(other(distance), sends, distance - 1)
    make(me, mine, me)
    pl.semaphore_wait(barrier, cells + lower.astype(jnp.int32) + upper.astype(jnp.int32))

    def a_copy(distance, owner):
        return remote(sends.at[distance - 1], mine.at[owner], a_sent.at[distance - 1],
                      a_landed.at[owner], {"cell": other(distance)})

    def v_copy(distance, owner):
        return remote(link_ref.at[0], links.at[owner], v_sent.at[distance - 1],
                      v_landed.at[owner], {"cell": other(distance)})

    for distance in ARRIVALS:
        a_copy(distance, me).start()

    @pl.when(me < cells - 1)
    def _():
        for distance in ARRIVALS:
            v_copy(distance, me).start()
        links[me] = link_ref[0]

    def wait_a(cell):
        @pl.when(me != cell)
        def _():
            a_copy(1, cell).wait_recv()
        return mine[cell, 0], mine[cell, 1]

    def wait_v(cell):
        @pl.when(me != cell)
        def _():
            v_copy(1, cell).wait_recv()
        return links[cell, 0], links[cell, 1]

    def x_send(cell):
        return remote(green_ref.at[cell], diag_ref.at[me], x_sent.at[cell], x_landed.at[me], {"cell": cell})

    def keep(cell, green):
        green_ref[cell, 0] = green[0]
        green_ref[cell, 1] = green[1]

    def ship(cell):
        @pl.when(me != cell)
        def _():
            x_send(cell).start()

    def x_copy(distance, slot):
        return remote(green_ref.at[other(distance)], diag_ref.at[slot], x_sent.at[distance - 1],
                      x_landed.at[slot], {"cell": other(distance)})

    def from_slot(step):
        return me if step == 0 else other(cells - ARRIVALS[step - 1])

    def source(step):
        return green_ref.at[me] if step == 0 else diag_ref.at[from_slot(step)]

    def up(step):
        slot = from_slot(step)
        return remote(source(step), near.at[0, slot], z_sent.at[0, step], landed.at[0, slot], {"energy": energy + 2})

    def down(step):
        slot = from_slot(step)
        return remote(source(step), near.at[3, slot], z_sent.at[1, step], landed.at[3, slot], {"energy": energy - 2})

    def across(step):
        slot = from_slot(step)
        return remote(source(step), near.at[1 + core, slot], z_sent.at[2, step], landed.at[1 + core, slot], {"energy": partner})

    def forward(step, sees, place):
        slot = from_slot(step)
        return remote(near.at[sees, slot], near.at[place, slot], f_sent.at[step], landed.at[place, slot], {"energy": partner})

    def arrived(side, step):
        slot = from_slot(step)
        remote(near.at[side, slot], near.at[side, slot], f_sent.at[step], landed.at[side, slot], {"energy": partner}).wait_recv()

    def send(step):
        @pl.when(upper)
        def _():
            up(step).start()

        @pl.when(lower)
        def _():
            down(step).start()
        across(step).start()

    def receive_x(step):
        distance = ARRIVALS[step - 1]
        x_copy(distance, other(cells - distance)).wait_recv()
        send(step)

    def relay(step):
        @pl.when(lower)
        def _():
            arrived(0, step)

            @pl.when(core == 1)
            def _():
                forward(step, 0, 1).start()

        @pl.when(upper)
        def _():
            arrived(3, step)

            @pl.when(core == 0)
            def _():
                forward(step, 3, 2).start()

    def finish(step):
        @pl.when(jnp.logical_or(core == 1, lower))
        def _():
            arrived(1, step)

        @pl.when(jnp.logical_or(core == 0, upper))
        def _():
            arrived(2, step)
        slot = from_slot(step)
        blocks = [near[0, slot], near[1, slot], diag_ref[slot], near[2, slot], near[3, slot]]
        for q in range(4):
            total = weights[q, step] * blocks[0]
            for o in range(1, 5):
                total += weights[q, 4 * o + step] * blocks[o]
            sigma_ref[q] = total if step == 0 else sigma_ref[q] + total

    zero = jnp.zeros(near.shape[1:], jnp.float32)

    @pl.when(jnp.logical_not(lower))
    def _():
        near[0] = zero

        @pl.when(core == 0)
        def _():
            near[1] = zero

    @pl.when(jnp.logical_not(upper))
    def _():
        near[3] = zero

        @pl.when(core == 1)
        def _():
            near[2] = zero

    def weigh(q, o, step):
        place = jnp.clip(4 * (energy + o - 2) + from_slot(step), 0, 4 * energies - 1)
        apart = jnp.abs(owner_ref[place] - owner_ref[4 * energy + q])
        terms = [jnp.where(apart == offsets_ref[m], strengths_ref[m], 0.0) for m in range(4)]
        weights[q, 4 * o + step] = (terms[0] + terms[1]) + (terms[2] + terms[3])

    for q in range(4):
        for o in range(5):
            for step in range(4):
                weigh(q, o, step)
    solve(wait_a, wait_v, keep)
    for cell in (1, 2, 0, 3):
        ship(cell)
    send(0)
    diag_ref[me] = green_ref[me]
    receive_x(1)
    receive_x(2)
    relay(0)
    receive_x(3)
    stores = [pltpu.make_async_copy(diag_ref, diag_out, stored.at[0])]
    stores[0].start()
    relay(1)
    finish(0)
    relay(2)
    finish(1)
    relay(3)
    finish(2)
    finish(3)
    stores.append(pltpu.make_async_copy(sigma_ref, sigma_out, stored.at[1]))
    stores[1].start()
    for cell in range(4):
        @pl.when(me != cell)
        def _():
            x_send(cell).wait_send()
    for step in range(4):
        @pl.when(upper)
        def _():
            up(step).wait_send()

        @pl.when(lower)
        def _():
            down(step).wait_send()
        across(step).wait_send()

        @pl.when(jnp.logical_and(core == 1, lower))
        def _():
            forward(step, 0, 1).wait_send()

        @pl.when(jnp.logical_and(core == 0, upper))
        def _():
            forward(step, 3, 2).wait_send()
    for distance in ARRIVALS:
        a_copy(distance, me).wait_send()

    @pl.when(me < cells - 1)
    def _():
        for distance in ARRIVALS:
            v_copy(distance, me).wait_send()
    for store in stores:
        store.wait()


def born(owner, hamiltonian, coupling, sigma_in, offsets, strengths):
    dma = pltpu.SemaphoreType.DMA
    shape = sigma_in.shape[1:]
    out = jax.ShapeDtypeStruct(shape, jnp.float32)
    buffer = lambda count: pltpu.VMEM((count,) + shape[1:], jnp.float32)
    whole = lambda x: pltpu.VMEM(x.shape, jnp.float32)
    return pl.pallas_call(
        born_kernel,
        out_shape=(out, out),
        in_specs=[pl.BlockSpec(memory_space=pltpu.HBM)] * 6,
        out_specs=(pl.BlockSpec(memory_space=pl.ANY),) * 2,
        scratch_shapes=[
            buffer(4), buffer(4), pltpu.SMEM(owner.shape, jnp.int32), whole(hamiltonian), whole(coupling), whole(sigma_in),
            pltpu.SMEM(offsets.shape, jnp.int32), pltpu.SMEM(strengths.shape, jnp.float32),
            buffer(3), buffer(4), buffer(3), pltpu.VMEM(shape[1:], jnp.float32),
            buffer(4), pltpu.VMEM((4,) + shape, jnp.float32), pltpu.SMEM((4, 20), jnp.float32),
            dma((6,)), dma((3,)), dma((4,)), dma((3,)), dma((3,)),
            dma((4,)), dma((4,)), dma((3, 4)), dma((4,)), dma((4, 4)), dma((2,)),
        ],
        compiler_params=pltpu.CompilerParams(collective_id=0, has_side_effects=True),
    )(owner, hamiltonian, coupling, sigma_in, offsets, strengths)


def write_kernel(diag_ref, sigma_ref, diag_out, sigma_out, held, read, written):
    pairs = [(source.at[slot], target.at[slot]) for source, target in ((diag_ref, diag_out), (sigma_ref, sigma_out)) for slot in range(4)]
    reads = [pltpu.make_async_copy(source, held.at[at], read.at[at]) for at, (source, target) in enumerate(pairs)]
    writes = [pltpu.make_async_copy(held.at[at], target, written.at[at]) for at, (source, target) in enumerate(pairs)]
    for copy in reads:
        copy.start()
    for copy, onward in zip(reads, writes):
        copy.wait()
        onward.start()
    for copy in writes:
        copy.wait()


def write(diag, sigma):
    shape = jax.ShapeDtypeStruct(diag.shape, jnp.float32)
    return pl.pallas_call(
        write_kernel,
        out_shape=(shape, shape),
        in_specs=[pl.BlockSpec(memory_space=pl.ANY)] * 2,
        out_specs=(pl.BlockSpec(memory_space=pl.ANY),) * 2,
        scratch_shapes=[
            pltpu.VMEM((8,) + diag.shape[1:], jnp.float32),
            pltpu.SemaphoreType.DMA((8,)), pltpu.SemaphoreType.DMA((8,)),
        ],
    )(diag, sigma)


def per_device(hamiltonian, coupling, sigma_in, mode_offsets, mode_coupling, energy_owner):
    green_diag, sigma_out = write(
        *born(energy_owner, hamiltonian, coupling, sigma_in, mode_offsets, mode_coupling))
    return (green_diag[None], sigma_out[None])


def solution(mesh):
    in_specs = (
        P("cell", None, None, None),
        P("cell", None, None, None),
        P("cell", "energy", None, None, None),
        P(),
        P(),
        P(),
    )
    out_specs = (P("cell", "energy", None, None, None), P("cell", "energy", None, None, None))
    return jax.shard_map(
        per_device, mesh=mesh, in_specs=in_specs, out_specs=out_specs, check_vma=False
    )
```

```python
import jax
import jax.numpy as jnp
from jax import lax
from jax.experimental import pallas as pl
from jax.experimental.pallas import tpu as pltpu
from jax.sharding import PartitionSpec as P

OFFSET_MAX = 8

BROADENING = 0.2
CONTACT_RATE = 0.5
LEAD_WIDTH = 1.0
BAND_LOW = -2.5
BAND_SPAN = 5.0
HALF = 64


def halves(x):
    high = x.astype(jnp.bfloat16)
    return high, (x - high.astype(jnp.float32)).astype(jnp.bfloat16)


def dot(x, y):
    once = lambda p, q: lax.dot_general(p, q, (((1,), (0,)), ((), ())), preferred_element_type=jnp.float32)
    (x_high, x_low), (y_high, y_low) = halves(x), halves(y)
    return once(x_high, y_high) + (once(x_high, y_low) + once(x_low, y_high))


def packed_sign(shape):
    li = lax.broadcasted_iota(jnp.int32, shape, 1)
    return jnp.where(li < HALF, -1.0, 1.0)

def rot(x):
    return pltpu.roll(x, HALF, 1) * packed_sign((1, 2 * HALF))

def pprod(x, y):
    return dot(x, jnp.concatenate([y, rot(y)], axis=0))

def leaves(blocks):
    n = HALF // 8
    li = lax.broadcasted_iota(jnp.int32, (8, 2 * HALF), 1)
    si = lax.broadcasted_iota(jnp.int32, (8, 2 * HALF), 0)
    sign = jnp.where(li < HALF, -1.0, 1.0)
    wide = lambda x: jnp.broadcast_to(x, (8, 2 * HALF))
    tiles = [[b[8 * t:8 * t + 8] for t in range(n)] for b in blocks]
    for g in range(n):
        base = 8 * g
        for rows in tiles:
            panel = rows[g]
            spun = pltpu.roll(panel, HALF, 1) * sign
            cr = [wide(panel[:, base + j:base + j + 1]) for j in range(8)]
            ci = [wide(panel[:, HALF + base + j:HALF + base + j + 1]) for j in range(8)]
            for k in range(8):
                pr, pi = wide(cr[k][k:k + 1]), wide(ci[k][k:k + 1])
                d = 1.0 / (pr * pr + pi * pi)
                ur, ui = cr[k] - jnp.where(si == k, 1.0, 0.0), ci[k]
                for j in range(k + 1, 8):
                    xr, xi = wide(cr[j][k:k + 1]), wide(ci[j][k:k + 1])
                    wr = xr * pr + xi * pi
                    wi = xi * pr - xr * pi
                    cr[j] = cr[j] - d * (ur * wr - ui * wi)
                    ci[j] = ci[j] - d * (ur * wi + ui * wr)
                row = wide(panel[k:k + 1]) + jnp.where(li == base + k, 1.0, 0.0)
                turn = wide(spun[k:k + 1]) + jnp.where(li == HALF + base + k, 1.0, 0.0)
                v = row * pr - turn * pi
                vt = turn * pr + row * pi
                panel = panel - d * (ur * v + ui * vt)
                spun = spun - d * (ur * vt - ui * v)
            full = panel + jnp.where(li == base + si, 1.0, 0.0)
            turned = spun + jnp.where(li == HALF + base + si, 1.0, 0.0)
            fr = [wide(full[j:j + 1]) for j in range(8)]
            ft = [wide(turned[j:j + 1]) for j in range(8)]
            near = [g + 1] if g + 1 < n else []
            far = [t for t in range(g + 2, n)] + [t for t in range(g)]
            for t in near:
                x = rows[t]
                terms = [wide(x[:, base + j:base + j + 1]) * fr[j] + wide(x[:, HALF + base + j:HALF + base + j + 1]) * ft[j] for j in range(8)]
                while len(terms) > 1:
                    terms = [p + q for p, q in zip(terms[::2], terms[1::2])]
                rows[t] = x - terms[0]
            empty = jnp.zeros_like(full)
            weight = jnp.concatenate([full if t == g else turned if t == g + n else empty for t in range(2 * n)], axis=0)
            moved = dot(jnp.concatenate([rows[t] for t in far], axis=0), weight)
            for at, t in enumerate(far):
                rows[t] = rows[t] - moved[8 * at:8 * at + 8]
            rows[g] = panel
    return [jnp.concatenate(rows, axis=0) for rows in tiles]

def quads(x):
    re, im = x
    def q(p, c):
        rows = slice(HALF * p, HALF * (p + 1)); cols = slice(HALF * c, HALF * (c + 1))
        return jnp.concatenate([re[rows, cols], im[rows, cols]], axis=1)
    return q(0, 0), q(0, 1), q(1, 0), q(1, 1)

def planes(qs):
    q00, q01, q10, q11 = qs
    re = jnp.concatenate([jnp.concatenate([q00[:, :HALF], q01[:, :HALF]], 1), jnp.concatenate([q10[:, :HALF], q11[:, :HALF]], 1)], 0)
    im = jnp.concatenate([jnp.concatenate([q00[:, HALF:], q01[:, HALF:]], 1), jnp.concatenate([q10[:, HALF:], q11[:, HALF:]], 1)], 0)
    return re, im

def invert_all(mats):
    qs = [quads(m) for m in mats]
    firsts = leaves([q[0] for q in qs])
    ts, ss, us = [], [], []
    for q, f in zip(qs, firsts):
        t = pprod(q[2], f)
        ts.append(t); us.append(pprod(f, q[1]))
        ss.append(q[3] - pprod(t, q[1]))
    seconds = leaves(ss)
    outs = []
    for f, t, u, s in zip(firsts, ts, us, seconds):
        lower = pprod(s, t)
        outs.append(planes((f + pprod(u, lower), -pprod(u, s), -lower, s)))
    return outs

def cprod(x, y):
    xr, xi = x; yr, yi = y
    lhs = jnp.concatenate([xr, xi], axis=1)
    rhs = jnp.concatenate([jnp.concatenate([yr, yi], 1), jnp.concatenate([-yi, yr], 1)], 0)
    out = dot(lhs, rhs)
    n = yr.shape[1]
    return out[:, :n], out[:, n:]

def adj(x):
    return x[0].T, -x[1].T

def add(x, y): return x[0] + y[0], x[1] + y[1]
def sub(x, y): return x[0] - y[0], x[1] - y[1]

def solve(block, link, keep):
    g0, g3 = invert_all([block(0), block(3)])
    v0, v2 = link(0), link(2)
    h0, h2 = adj(v0), adj(v2)
    t0 = cprod(g0, v0)
    u3 = cprod(g3, h2)
    d2 = sub(block(2), cprod(v2, u3))
    g2, = invert_all([d2])
    d1 = sub(block(1), cprod(h0, t0))
    v1 = link(1)
    w = cprod(g2, adj(v1))
    y2 = cprod(v1, g2)
    y0 = cprod(h0, g0)
    x3 = cprod(v2, g3)
    base3 = add(g3, cprod(u3, cprod(g2, x3)))
    y3 = cprod(y2, x3)
    w3 = cprod(u3, w)
    green1, = invert_all([sub(d1, cprod(v1, w))])
    keep(1, green1)
    keep(2, add(g2, cprod(w, cprod(green1, y2))))
    keep(0, add(g0, cprod(t0, cprod(green1, y0))))
    keep(3, add(base3, cprod(w3, cprod(green1, y3))))


MESH = pl.DeviceIdType.MESH
ARRIVALS = (1, 3, 2)


def remote(source, target, sent, landed, where):
    return pltpu.make_async_remote_copy(
        src_ref=source, dst_ref=target, send_sem=sent, recv_sem=landed,
        device_id=where, device_id_type=MESH,
    )


def born_kernel(owner_hbm, ham_hbm, link_hbm, self_hbm, offsets_hbm, strengths_hbm, diag_out, sigma_out,
                diag_ref, sigma_ref, owner_ref, ham_ref, link_ref, self_ref, offsets_ref, strengths_ref, sends, mine, links, fold,
                green_ref, near, weights, loaded, a_sent, a_landed, v_sent, v_landed,
                x_sent, x_landed, z_sent, f_sent, landed, stored):
    loads = [
        pltpu.make_async_copy(source, target, loaded.at[at])
        for at, (source, target) in enumerate(
            ((owner_hbm, owner_ref), (ham_hbm, ham_ref), (link_hbm, link_ref), (self_hbm, self_ref),
             (offsets_hbm, offsets_ref), (strengths_hbm, strengths_ref)))
    ]
    for load in loads:
        load.start()
    cells, slots = 4, 4
    me = lax.axis_index("cell")
    energy = lax.axis_index("energy")
    energies = lax.axis_size("energy")
    last = slots * energies - 1
    core = lax.rem(energy, 2)
    partner = energy + 1 - 2 * core
    lower, upper = energy >= 2, energy < energies - 2
    other = lambda distance: lax.rem(me + distance, cells)
    barrier = pltpu.get_barrier_semaphore()
    def greet(where):
        pl.semaphore_signal(barrier, 1, device_id=where, device_id_type=MESH)

    for distance in ARRIVALS:
        greet({"cell": other(distance)})
    greet({"energy": partner})

    @pl.when(lower)
    def _():
        greet({"energy": energy - 2})

    @pl.when(upper)
    def _():
        greet({"energy": energy + 2})
    side = fold.shape[-1]
    eye = jnp.where(
        lax.broadcasted_iota(jnp.int32, (side, side), 0) == lax.broadcasted_iota(jnp.int32, (side, side), 1), 1.0, 0.0)
    at_start = jnp.where(me == 0, CONTACT_RATE, 0.0)
    for load in loads:
        load.wait()
    fold[0] = -ham_ref[0, 0]
    fold[1] = (BROADENING + at_start) * eye - ham_ref[0, 1]

    @pl.when(me == cells - 1)
    def _():
        link = link_ref[0, 0], link_ref[0, 1]
        beyond = cprod(link, adj(link))
        fold[0] = fold[0] - LEAD_WIDTH * beyond[1]
        fold[1] = fold[1] + LEAD_WIDTH * beyond[0]

    def make(slot, target, at):
        index = jnp.full((1, side), owner_ref[slots * energy + slot], jnp.int32)
        level = BAND_LOW + BAND_SPAN * index.astype(jnp.float32) / last
        target[at, 0] = level * eye + fold[0] - self_ref[0, slot, 0]
        target[at, 1] = fold[1] - self_ref[0, slot, 1]

    for distance in ARRIVALS:
        make(other(distance), sends, distance - 1)
    make(me, mine, me)
    pl.semaphore_wait(barrier, cells + lower.astype(jnp.int32) + upper.astype(jnp.int32))

    def a_copy(distance, owner):
        return remote(sends.at[distance - 1], mine.at[owner], a_sent.at[distance - 1],
                      a_landed.at[owner], {"cell": other(distance)})

    def v_copy(distance, owner):
        return remote(link_ref.at[0], links.at[owner], v_sent.at[distance - 1],
                      v_landed.at[owner], {"cell": other(distance)})

    for distance in ARRIVALS:
        a_copy(distance, me).start()

    @pl.when(me < cells - 1)
    def _():
        for distance in ARRIVALS:
            v_copy(distance, me).start()
        links[me] = link_ref[0]

    def wait_a(cell):
        @pl.when(me != cell)
        def _():
            a_copy(1, cell).wait_recv()
        return mine[cell, 0], mine[cell, 1]

    def wait_v(cell):
        @pl.when(me != cell)
        def _():
            v_copy(1, cell).wait_recv()
        return links[cell, 0], links[cell, 1]

    def x_send(cell):
        return remote(green_ref.at[cell], diag_ref.at[me], x_sent.at[cell], x_landed.at[me], {"cell": cell})

    def keep(cell, green):
        green_ref[cell, 0] = green[0]
        green_ref[cell, 1] = green[1]

    def ship(cell):
        @pl.when(me != cell)
        def _():
            x_send(cell).start()

    def x_copy(distance, slot):
        return remote(green_ref.at[other(distance)], diag_ref.at[slot], x_sent.at[distance - 1],
                      x_landed.at[slot], {"cell": other(distance)})

    def from_slot(step):
        return me if step == 0 else other(cells - ARRIVALS[step - 1])

    def source(step):
        return green_ref.at[me] if step == 0 else diag_ref.at[from_slot(step)]

    def up(step):
        slot = from_slot(step)
        return remote(source(step), near.at[0, slot], z_sent.at[0, step], landed.at[0, slot], {"energy": energy + 2})

    def down(step):
        slot = from_slot(step)
        return remote(source(step), near.at[3, slot], z_sent.at[1, step], landed.at[3, slot], {"energy": energy - 2})

    def across(step):
        slot = from_slot(step)
        return remote(source(step), near.at[1 + core, slot], z_sent.at[2, step], landed.at[1 + core, slot], {"energy": partner})

    def forward(step, sees, place):
        slot = from_slot(step)
        return remote(near.at[sees, slot], near.at[place, slot], f_sent.at[step], landed.at[place, slot], {"energy": partner})

    def arrived(side, step):
        slot = from_slot(step)
        remote(near.at[side, slot], near.at[side, slot], f_sent.at[step], landed.at[side, slot], {"energy": partner}).wait_recv()

    def send(step):
        @pl.when(upper)
        def _():
            up(step).start()

        @pl.when(lower)
        def _():
            down(step).start()
        across(step).start()

    def receive_x(step):
        distance = ARRIVALS[step - 1]
        x_copy(distance, other(cells - distance)).wait_recv()
        send(step)

    def relay(step):
        @pl.when(lower)
        def _():
            arrived(0, step)

            @pl.when(core == 1)
            def _():
                forward(step, 0, 1).start()

        @pl.when(upper)
        def _():
            arrived(3, step)

            @pl.when(core == 0)
            def _():
                forward(step, 3, 2).start()

    def finish(step):
        @pl.when(jnp.logical_or(core == 1, lower))
        def _():
            arrived(1, step)

        @pl.when(jnp.logical_or(core == 0, upper))
        def _():
            arrived(2, step)
        slot = from_slot(step)
        blocks = [near[0, slot], near[1, slot], diag_ref[slot], near[2, slot], near[3, slot]]
        for q in range(4):
            total = weights[q, step] * blocks[0]
            for o in range(1, 5):
                total += weights[q, 4 * o + step] * blocks[o]
            sigma_ref[q] = total if step == 0 else sigma_ref[q] + total

    zero = jnp.zeros(near.shape[1:], jnp.float32)

    @pl.when(jnp.logical_not(lower))
    def _():
        near[0] = zero

        @pl.when(core == 0)
        def _():
            near[1] = zero

    @pl.when(jnp.logical_not(upper))
    def _():
        near[3] = zero

        @pl.when(core == 1)
        def _():
            near[2] = zero

    def weigh(q, o, step):
        place = jnp.clip(4 * (energy + o - 2) + from_slot(step), 0, 4 * energies - 1)
        apart = jnp.abs(owner_ref[place] - owner_ref[4 * energy + q])
        terms = [jnp.where(apart == offsets_ref[m], strengths_ref[m], 0.0) for m in range(4)]
        weights[q, 4 * o + step] = (terms[0] + terms[1]) + (terms[2] + terms[3])

    for q in range(4):
        for o in range(5):
            for step in range(4):
                weigh(q, o, step)
    solve(wait_a, wait_v, keep)
    for cell in (1, 2, 0, 3):
        ship(cell)
    send(0)
    diag_ref[me] = green_ref[me]
    receive_x(1)
    receive_x(2)
    relay(0)
    receive_x(3)
    stores = [pltpu.make_async_copy(diag_ref, diag_out, stored.at[0])]
    stores[0].start()
    relay(1)
    finish(0)
    relay(2)
    finish(1)
    relay(3)
    finish(2)
    finish(3)
    stores.append(pltpu.make_async_copy(sigma_ref, sigma_out, stored.at[1]))
    stores[1].start()
    for cell in range(4):
        @pl.when(me != cell)
        def _():
            x_send(cell).wait_send()
    for step in range(4):
        @pl.when(upper)
        def _():
            up(step).wait_send()

        @pl.when(lower)
        def _():
            down(step).wait_send()
        across(step).wait_send()

        @pl.when(jnp.logical_and(core == 1, lower))
        def _():
            forward(step, 0, 1).wait_send()

        @pl.when(jnp.logical_and(core == 0, upper))
        def _():
            forward(step, 3, 2).wait_send()
    for distance in ARRIVALS:
        a_copy(distance, me).wait_send()

    @pl.when(me < cells - 1)
    def _():
        for distance in ARRIVALS:
            v_copy(distance, me).wait_send()
    for store in stores:
        store.wait()


def born(owner, hamiltonian, coupling, sigma_in, offsets, strengths):
    dma = pltpu.SemaphoreType.DMA
    shape = sigma_in.shape[1:]
    out = jax.ShapeDtypeStruct(shape, jnp.float32)
    buffer = lambda count: pltpu.VMEM((count,) + shape[1:], jnp.float32)
    whole = lambda x: pltpu.VMEM(x.shape, jnp.float32)
    return pl.pallas_call(
        born_kernel,
        out_shape=(out, out),
        in_specs=[pl.BlockSpec(memory_space=pltpu.HBM)] * 6,
        out_specs=(pl.BlockSpec(memory_space=pl.ANY),) * 2,
        scratch_shapes=[
            buffer(4), buffer(4), pltpu.SMEM(owner.shape, jnp.int32), whole(hamiltonian), whole(coupling), whole(sigma_in),
            pltpu.SMEM(offsets.shape, jnp.int32), pltpu.SMEM(strengths.shape, jnp.float32),
            buffer(3), buffer(4), buffer(3), pltpu.VMEM(shape[1:], jnp.float32),
            buffer(4), pltpu.VMEM((4,) + shape, jnp.float32), pltpu.SMEM((4, 20), jnp.float32),
            dma((6,)), dma((3,)), dma((4,)), dma((3,)), dma((3,)),
            dma((4,)), dma((4,)), dma((3, 4)), dma((4,)), dma((4, 4)), dma((2,)),
        ],
        compiler_params=pltpu.CompilerParams(collective_id=0, has_side_effects=True),
    )(owner, hamiltonian, coupling, sigma_in, offsets, strengths)


def write_kernel(diag_ref, sigma_ref, diag_out, sigma_out, held, read, written):
    pairs = [(source.at[slot], target.at[slot]) for source, target in ((diag_ref, diag_out), (sigma_ref, sigma_out)) for slot in range(4)]
    reads = [pltpu.make_async_copy(source, held.at[at], read.at[at]) for at, (source, target) in enumerate(pairs)]
    writes = [pltpu.make_async_copy(held.at[at], target, written.at[at]) for at, (source, target) in enumerate(pairs)]
    for copy in reads:
        copy.start()
    for copy, onward in zip(reads, writes):
        copy.wait()
        onward.start()
    for copy in writes:
        copy.wait()


def write(diag, sigma):
    shape = jax.ShapeDtypeStruct(diag.shape, jnp.float32)
    return pl.pallas_call(
        write_kernel,
        out_shape=(shape, shape),
        in_specs=[pl.BlockSpec(memory_space=pl.ANY)] * 2,
        out_specs=(pl.BlockSpec(memory_space=pl.ANY),) * 2,
        scratch_shapes=[
            pltpu.VMEM((8,) + diag.shape[1:], jnp.float32),
            pltpu.SemaphoreType.DMA((8,)), pltpu.SemaphoreType.DMA((8,)),
        ],
    )(diag, sigma)


def per_device(hamiltonian, coupling, sigma_in, mode_offsets, mode_coupling, energy_owner):
    green_diag, sigma_out = write(
        *born(energy_owner, hamiltonian, coupling, sigma_in, mode_offsets, mode_coupling))
    return (green_diag[None], sigma_out[None])


def solution(mesh):
    in_specs = (
        P("cell", None, None, None),
        P("cell", None, None, None),
        P("cell", "energy", None, None, None),
        P(),
        P(),
        P(),
    )
    out_specs = (P("cell", "energy", None, None, None), P("cell", "energy", None, None, None))
    return jax.shard_map(
        per_device, mesh=mesh, in_specs=in_specs, out_specs=out_specs, check_vma=False
    )
```

```python
import jax
import jax.numpy as jnp
from jax import lax
from jax.experimental import pallas as pl
from jax.experimental.pallas import tpu as pltpu
from jax.sharding import PartitionSpec as P

OFFSET_MAX = 8

BROADENING = 0.2
CONTACT_RATE = 0.5
LEAD_WIDTH = 1.0
BAND_LOW = -2.5
BAND_SPAN = 5.0
HALF = 64


def halves(x):
    high = x.astype(jnp.bfloat16)
    return high, (x - high.astype(jnp.float32)).astype(jnp.bfloat16)


def dot(x, y):
    once = lambda p, q: lax.dot_general(p, q, (((1,), (0,)), ((), ())), preferred_element_type=jnp.float32)
    (x_high, x_low), (y_high, y_low) = halves(x), halves(y)
    return once(x_high, y_high) + (once(x_high, y_low) + once(x_low, y_high))


def packed_sign(shape):
    li = lax.broadcasted_iota(jnp.int32, shape, 1)
    return jnp.where(li < HALF, -1.0, 1.0)

def rot(x):
    return pltpu.roll(x, HALF, 1) * packed_sign((1, 2 * HALF))

def pprod(x, y):
    return dot(x, jnp.concatenate([y, rot(y)], axis=0))

def leaves(blocks):
    n = HALF // 8
    li = lax.broadcasted_iota(jnp.int32, (8, 2 * HALF), 1)
    si = lax.broadcasted_iota(jnp.int32, (8, 2 * HALF), 0)
    sign = jnp.where(li < HALF, -1.0, 1.0)
    wide = lambda x: jnp.broadcast_to(x, (8, 2 * HALF))
    tiles = [[b[8 * t:8 * t + 8] for t in range(n)] for b in blocks]
    for g in range(n):
        base = 8 * g
        for rows in tiles:
            panel = rows[g]
            spun = pltpu.roll(panel, HALF, 1) * sign
            cr = [wide(panel[:, base + j:base + j + 1]) for j in range(8)]
            ci = [wide(panel[:, HALF + base + j:HALF + base + j + 1]) for j in range(8)]
            for k in range(8):
                pr, pi = wide(cr[k][k:k + 1]), wide(ci[k][k:k + 1])
                d = 1.0 / (pr * pr + pi * pi)
                ur, ui = cr[k] - jnp.where(si == k, 1.0, 0.0), ci[k]
                for j in range(k + 1, 8):
                    xr, xi = wide(cr[j][k:k + 1]), wide(ci[j][k:k + 1])
                    wr = xr * pr + xi * pi
                    wi = xi * pr - xr * pi
                    cr[j] = cr[j] - d * (ur * wr - ui * wi)
                    ci[j] = ci[j] - d * (ur * wi + ui * wr)
                row = wide(panel[k:k + 1]) + jnp.where(li == base + k, 1.0, 0.0)
                turn = wide(spun[k:k + 1]) + jnp.where(li == HALF + base + k, 1.0, 0.0)
                v = row * pr - turn * pi
                vt = turn * pr + row * pi
                panel = panel - d * (ur * v + ui * vt)
                spun = spun - d * (ur * vt - ui * v)
            full = panel + jnp.where(li == base + si, 1.0, 0.0)
            turned = spun + jnp.where(li == HALF + base + si, 1.0, 0.0)
            fr = [wide(full[j:j + 1]) for j in range(8)]
            ft = [wide(turned[j:j + 1]) for j in range(8)]
            near = [g + 1] if g + 1 < n else []
            far = [t for t in range(g + 2, n)] + [t for t in range(g)]
            for t in near:
                x = rows[t]
                terms = [wide(x[:, base + j:base + j + 1]) * fr[j] + wide(x[:, HALF + base + j:HALF + base + j + 1]) * ft[j] for j in range(8)]
                while len(terms) > 1:
                    terms = [p + q for p, q in zip(terms[::2], terms[1::2])]
                rows[t] = x - terms[0]
            empty = jnp.zeros_like(full)
            weight = jnp.concatenate([full if t == g else turned if t == g + n else empty for t in range(2 * n)], axis=0)
            moved = dot(jnp.concatenate([rows[t] for t in far], axis=0), weight)
            for at, t in enumerate(far):
                rows[t] = rows[t] - moved[8 * at:8 * at + 8]
            rows[g] = panel
    return [jnp.concatenate(rows, axis=0) for rows in tiles]

def quads(x):
    re, im = x
    def q(p, c):
        rows = slice(HALF * p, HALF * (p + 1)); cols = slice(HALF * c, HALF * (c + 1))
        return jnp.concatenate([re[rows, cols], im[rows, cols]], axis=1)
    return q(0, 0), q(0, 1), q(1, 0), q(1, 1)

def planes(qs):
    q00, q01, q10, q11 = qs
    re = jnp.concatenate([jnp.concatenate([q00[:, :HALF], q01[:, :HALF]], 1), jnp.concatenate([q10[:, :HALF], q11[:, :HALF]], 1)], 0)
    im = jnp.concatenate([jnp.concatenate([q00[:, HALF:], q01[:, HALF:]], 1), jnp.concatenate([q10[:, HALF:], q11[:, HALF:]], 1)], 0)
    return re, im

def invert_all(mats):
    qs = [quads(m) for m in mats]
    firsts = leaves([q[0] for q in qs])
    ts, ss, us = [], [], []
    for q, f in zip(qs, firsts):
        t = pprod(q[2], f)
        ts.append(t); us.append(pprod(f, q[1]))
        ss.append(q[3] - pprod(t, q[1]))
    seconds = leaves(ss)
    outs = []
    for f, t, u, s in zip(firsts, ts, us, seconds):
        lower = pprod(s, t)
        outs.append(planes((f + pprod(u, lower), -pprod(u, s), -lower, s)))
    return outs

def cprod(x, y):
    xr, xi = x; yr, yi = y
    lhs = jnp.concatenate([xr, xi], axis=1)
    rhs = jnp.concatenate([jnp.concatenate([yr, yi], 1), jnp.concatenate([-yi, yr], 1)], 0)
    out = dot(lhs, rhs)
    n = yr.shape[1]
    return out[:, :n], out[:, n:]

def adj(x):
    return x[0].T, -x[1].T

def add(x, y): return x[0] + y[0], x[1] + y[1]
def sub(x, y): return x[0] - y[0], x[1] - y[1]

def solve(block, link, keep):
    g0, g3 = invert_all([block(0), block(3)])
    v0, v2 = link(0), link(2)
    h0, h2 = adj(v0), adj(v2)
    t0 = cprod(g0, v0)
    u3 = cprod(g3, h2)
    d2 = sub(block(2), cprod(v2, u3))
    g2, = invert_all([d2])
    d1 = sub(block(1), cprod(h0, t0))
    v1 = link(1)
    w = cprod(g2, adj(v1))
    y2 = cprod(v1, g2)
    y0 = cprod(h0, g0)
    x3 = cprod(v2, g3)
    base3 = add(g3, cprod(u3, cprod(g2, x3)))
    y3 = cprod(y2, x3)
    w3 = cprod(u3, w)
    green1, = invert_all([sub(d1, cprod(v1, w))])
    keep(1, green1)
    keep(2, add(g2, cprod(w, cprod(green1, y2))))
    keep(0, add(g0, cprod(t0, cprod(green1, y0))))
    keep(3, add(base3, cprod(w3, cprod(green1, y3))))


MESH = pl.DeviceIdType.MESH
ARRIVALS = (1, 3, 2)


def remote(source, target, sent, landed, where):
    return pltpu.make_async_remote_copy(
        src_ref=source, dst_ref=target, send_sem=sent, recv_sem=landed,
        device_id=where, device_id_type=MESH,
    )


def born_kernel(owner_hbm, ham_hbm, link_hbm, self_hbm, offsets_hbm, strengths_hbm, diag_out, sigma_out,
                diag_ref, sigma_ref, owner_ref, ham_ref, link_ref, self_ref, offsets_ref, strengths_ref, sends, mine, links, fold,
                green_ref, near, weights, loaded, a_sent, a_landed, v_sent, v_landed,
                x_sent, x_landed, z_sent, f_sent, landed, stored):
    loads = [
        pltpu.make_async_copy(source, target, loaded.at[at])
        for at, (source, target) in enumerate(
            ((owner_hbm, owner_ref), (ham_hbm, ham_ref), (link_hbm, link_ref), (self_hbm, self_ref),
             (offsets_hbm, offsets_ref), (strengths_hbm, strengths_ref)))
    ]
    for load in loads:
        load.start()
    cells, slots = 4, 4
    me = lax.axis_index("cell")
    energy = lax.axis_index("energy")
    energies = lax.axis_size("energy")
    last = slots * energies - 1
    core = lax.rem(energy, 2)
    partner = energy + 1 - 2 * core
    lower, upper = energy >= 2, energy < energies - 2
    other = lambda distance: lax.rem(me + distance, cells)
    barrier = pltpu.get_barrier_semaphore()
    def greet(where):
        pl.semaphore_signal(barrier, 1, device_id=where, device_id_type=MESH)

    for distance in ARRIVALS:
        greet({"cell": other(distance)})
    greet({"energy": partner})

    @pl.when(lower)
    def _():
        greet({"energy": energy - 2})

    @pl.when(upper)
    def _():
        greet({"energy": energy + 2})
    side = fold.shape[-1]
    eye = jnp.where(
        lax.broadcasted_iota(jnp.int32, (side, side), 0) == lax.broadcasted_iota(jnp.int32, (side, side), 1), 1.0, 0.0)
    at_start = jnp.where(me == 0, CONTACT_RATE, 0.0)
    for load in loads:
        load.wait()
    fold[0] = -ham_ref[0, 0]
    fold[1] = (BROADENING + at_start) * eye - ham_ref[0, 1]

    @pl.when(me == cells - 1)
    def _():
        link = link_ref[0, 0], link_ref[0, 1]
        beyond = cprod(link, adj(link))
        fold[0] = fold[0] - LEAD_WIDTH * beyond[1]
        fold[1] = fold[1] + LEAD_WIDTH * beyond[0]

    def make(slot, target, at):
        index = jnp.full((1, side), owner_ref[slots * energy + slot], jnp.int32)
        level = BAND_LOW + BAND_SPAN * index.astype(jnp.float32) / last
        target[at, 0] = level * eye + fold[0] - self_ref[0, slot, 0]
        target[at, 1] = fold[1] - self_ref[0, slot, 1]

    for distance in ARRIVALS:
        make(other(distance), sends, distance - 1)
    make(me, mine, me)
    pl.semaphore_wait(barrier, cells + lower.astype(jnp.int32) + upper.astype(jnp.int32))

    def a_copy(distance, owner):
        return remote(sends.at[distance - 1], mine.at[owner], a_sent.at[distance - 1],
                      a_landed.at[owner], {"cell": other(distance)})

    def v_copy(distance, owner):
        return remote(link_ref.at[0], links.at[owner], v_sent.at[distance - 1],
                      v_landed.at[owner], {"cell": other(distance)})

    for distance in ARRIVALS:
        a_copy(distance, me).start()

    @pl.when(me < cells - 1)
    def _():
        for distance in ARRIVALS:
            v_copy(distance, me).start()
        links[me] = link_ref[0]

    def wait_a(cell):
        @pl.when(me != cell)
        def _():
            a_copy(1, cell).wait_recv()
        return mine[cell, 0], mine[cell, 1]

    def wait_v(cell):
        @pl.when(me != cell)
        def _():
            v_copy(1, cell).wait_recv()
        return links[cell, 0], links[cell, 1]

    def keep(cell, green):
        green_ref[cell, 0] = green[0]
        green_ref[cell, 1] = green[1]

    def x_copy(distance, slot):
        return remote(green_ref.at[other(distance)], diag_ref.at[slot], x_sent.at[distance - 1],
                      x_landed.at[slot], {"cell": other(distance)})

    def from_slot(step):
        return me if step == 0 else other(cells - ARRIVALS[step - 1])

    def source(step):
        return green_ref.at[me] if step == 0 else diag_ref.at[from_slot(step)]

    def up(step):
        slot = from_slot(step)
        return remote(source(step), near.at[0, slot], z_sent.at[0, step], landed.at[0, slot], {"energy": energy + 2})

    def down(step):
        slot = from_slot(step)
        return remote(source(step), near.at[3, slot], z_sent.at[1, step], landed.at[3, slot], {"energy": energy - 2})

    def across(step):
        slot = from_slot(step)
        return remote(source(step), near.at[1 + core, slot], z_sent.at[2, step], landed.at[1 + core, slot], {"energy": partner})

    def forward(step, sees, place):
        slot = from_slot(step)
        return remote(near.at[sees, slot], near.at[place, slot], f_sent.at[step], landed.at[place, slot], {"energy": partner})

    def arrived(side, step):
        slot = from_slot(step)
        remote(near.at[side, slot], near.at[side, slot], f_sent.at[step], landed.at[side, slot], {"energy": partner}).wait_recv()

    def send(step):
        @pl.when(upper)
        def _():
            up(step).start()

        @pl.when(lower)
        def _():
            down(step).start()
        across(step).start()

    def receive_x(step):
        distance = ARRIVALS[step - 1]
        x_copy(distance, other(cells - distance)).wait_recv()
        send(step)

    def relay(step):
        @pl.when(lower)
        def _():
            arrived(0, step)

            @pl.when(core == 1)
            def _():
                forward(step, 0, 1).start()

        @pl.when(upper)
        def _():
            arrived(3, step)

            @pl.when(core == 0)
            def _():
                forward(step, 3, 2).start()

    def finish(step):
        @pl.when(jnp.logical_or(core == 1, lower))
        def _():
            arrived(1, step)

        @pl.when(jnp.logical_or(core == 0, upper))
        def _():
            arrived(2, step)
        slot = from_slot(step)
        blocks = [near[0, slot], near[1, slot], diag_ref[slot], near[2, slot], near[3, slot]]
        for q in range(4):
            total = weights[q, step] * blocks[0]
            for o in range(1, 5):
                total += weights[q, 4 * o + step] * blocks[o]
            sigma_ref[q] = total if step == 0 else sigma_ref[q] + total

    zero = jnp.zeros(near.shape[1:], jnp.float32)

    @pl.when(jnp.logical_not(lower))
    def _():
        near[0] = zero

        @pl.when(core == 0)
        def _():
            near[1] = zero

    @pl.when(jnp.logical_not(upper))
    def _():
        near[3] = zero

        @pl.when(core == 1)
        def _():
            near[2] = zero

    def weigh(q, o, step):
        place = jnp.clip(4 * (energy + o - 2) + from_slot(step), 0, 4 * energies - 1)
        apart = jnp.abs(owner_ref[place] - owner_ref[4 * energy + q])
        terms = [jnp.where(apart == offsets_ref[m], strengths_ref[m], 0.0) for m in range(4)]
        weights[q, 4 * o + step] = (terms[0] + terms[1]) + (terms[2] + terms[3])

    for q in range(4):
        for o in range(5):
            for step in range(4):
                weigh(q, o, step)
    solve(wait_a, wait_v, keep)
    for distance in ARRIVALS:
        x_copy(distance, me).start()
    send(0)
    diag_ref[me] = green_ref[me]
    receive_x(1)
    receive_x(2)
    relay(0)
    receive_x(3)
    stores = [pltpu.make_async_copy(diag_ref, diag_out, stored.at[0])]
    stores[0].start()
    relay(1)
    finish(0)
    relay(2)
    finish(1)
    relay(3)
    finish(2)
    finish(3)
    stores.append(pltpu.make_async_copy(sigma_ref, sigma_out, stored.at[1]))
    stores[1].start()
    for distance in ARRIVALS:
        x_copy(distance, me).wait_send()
    for step in range(4):
        @pl.when(upper)
        def _():
            up(step).wait_send()

        @pl.when(lower)
        def _():
            down(step).wait_send()
        across(step).wait_send()

        @pl.when(jnp.logical_and(core == 1, lower))
        def _():
            forward(step, 0, 1).wait_send()

        @pl.when(jnp.logical_and(core == 0, upper))
        def _():
            forward(step, 3, 2).wait_send()
    for distance in ARRIVALS:
        a_copy(distance, me).wait_send()

    @pl.when(me < cells - 1)
    def _():
        for distance in ARRIVALS:
            v_copy(distance, me).wait_send()
    for store in stores:
        store.wait()


def born(owner, hamiltonian, coupling, sigma_in, offsets, strengths):
    dma = pltpu.SemaphoreType.DMA
    shape = sigma_in.shape[1:]
    out = jax.ShapeDtypeStruct(shape, jnp.float32)
    buffer = lambda count: pltpu.VMEM((count,) + shape[1:], jnp.float32)
    whole = lambda x: pltpu.VMEM(x.shape, jnp.float32)
    return pl.pallas_call(
        born_kernel,
        out_shape=(out, out),
        in_specs=[pl.BlockSpec(memory_space=pltpu.HBM)] * 6,
        out_specs=(pl.BlockSpec(memory_space=pl.ANY),) * 2,
        scratch_shapes=[
            buffer(4), buffer(4), pltpu.SMEM(owner.shape, jnp.int32), whole(hamiltonian), whole(coupling), whole(sigma_in),
            pltpu.SMEM(offsets.shape, jnp.int32), pltpu.SMEM(strengths.shape, jnp.float32),
            buffer(3), buffer(4), buffer(3), pltpu.VMEM(shape[1:], jnp.float32),
            buffer(4), pltpu.VMEM((4,) + shape, jnp.float32), pltpu.SMEM((4, 20), jnp.float32),
            dma((6,)), dma((3,)), dma((4,)), dma((3,)), dma((3,)),
            dma((3,)), dma((4,)), dma((3, 4)), dma((4,)), dma((4, 4)), dma((2,)),
        ],
        compiler_params=pltpu.CompilerParams(collective_id=0, has_side_effects=True),
    )(owner, hamiltonian, coupling, sigma_in, offsets, strengths)


def write_kernel(diag_ref, sigma_ref, diag_out, sigma_out, held, read, written):
    pairs = [(source.at[slot], target.at[slot]) for source, target in ((diag_ref, diag_out), (sigma_ref, sigma_out)) for slot in range(4)]
    reads = [pltpu.make_async_copy(source, held.at[at], read.at[at]) for at, (source, target) in enumerate(pairs)]
    writes = [pltpu.make_async_copy(held.at[at], target, written.at[at]) for at, (source, target) in enumerate(pairs)]
    for copy in reads:
        copy.start()
    for copy, onward in zip(reads, writes):
        copy.wait()
        onward.start()
    for copy in writes:
        copy.wait()


def write(diag, sigma):
    shape = jax.ShapeDtypeStruct(diag.shape, jnp.float32)
    return pl.pallas_call(
        write_kernel,
        out_shape=(shape, shape),
        in_specs=[pl.BlockSpec(memory_space=pl.ANY)] * 2,
        out_specs=(pl.BlockSpec(memory_space=pl.ANY),) * 2,
        scratch_shapes=[
            pltpu.VMEM((8,) + diag.shape[1:], jnp.float32),
            pltpu.SemaphoreType.DMA((8,)), pltpu.SemaphoreType.DMA((8,)),
        ],
    )(diag, sigma)


def per_device(hamiltonian, coupling, sigma_in, mode_offsets, mode_coupling, energy_owner):
    green_diag, sigma_out = write(
        *born(energy_owner, hamiltonian, coupling, sigma_in, mode_offsets, mode_coupling))
    return (green_diag[None], sigma_out[None])


def solution(mesh):
    in_specs = (
        P("cell", None, None, None),
        P("cell", None, None, None),
        P("cell", "energy", None, None, None),
        P(),
        P(),
        P(),
    )
    out_specs = (P("cell", "energy", None, None, None), P("cell", "energy", None, None, None))
    return jax.shard_map(
        per_device, mesh=mesh, in_specs=in_specs, out_specs=out_specs, check_vma=False
    )
```
